32 devices in a mesh: parts: 2 (over y), ep: 4 (over z), fs: 4 (over x, core).
Axes of the slice: x: 2, y: 2, z: 4, core: 2. Of those that a mesh axis runs over, the one named last changes fastest.
Arguments:
- hidden_states: bfloat16 [8, 512, 1152], P(('parts', 'fs'), 'ep'), parts along dimension 0, may hold values from -6 to 6
- expert_ids: int32 [8, 512, 2], P(('parts', 'fs'), 'ep'), parts along dimension 0, may hold values from 0 to 15, all different within a row; in each aligned block of 128 rows (0 to 127, 128 to 255, ..., all dimensions but the last counted through in order) at most 20 rows name the same one
- modulation: float32 [8, 3, 1152], P(('parts', 'fs')), parts along dimension 0, may hold values from -4 to 4
- router_weight: bfloat16 [1152, 16], replicated, may hold values from -0.1875 to 0.1875
- w_in: bfloat16 [32, 1152, 2304], P('ep', 'fs'), may hold values from -0.1875 to 0.1875
- b_in: float32 [32, 2304], P('ep'), may hold values from -3 to 3
- w_out: bfloat16 [32, 2304, 1152], P('ep', 'fs'), may hold values from -0.09375 to 0.09375
Outputs:
- layer_out: bfloat16 [8, 512, 1152], P(('parts', 'fs'), 'ep'), parts along dimension 0
The draws below stay inside these ranges and needn't reach their ends.
There are 2 independent parts, one for each index of `parts`. The reference program is written for one: setup_inputs(seed, part) draws one part's arguments, and reference() takes and returns one part's arrays. A program takes and returns all parts, laid end to end along the dimension named above; an argument that names none is the same for every part. Nothing has to cross between parts.
Inputs may be any that keep to these rules, and one draw needn't show every extreme that they name: `expert_ids`: the two ids of a token differ. In each aligned block of 128 tokens of an image, no expert is named by more than 20 tokens, a bound that some block reaches.
All inputs are finite; a program needn't handle non-finite values.
Results may differ from the reference program's by a relative error of at most 0.0046.
Values may be sent and summed in bfloat16 or wider, within the bound.
A program may use at most 192 MiB of HBM per device.

```python
import math
import jax
import jax.numpy as jnp
import numpy as np
from jax import lax

D = 1152
FF = 4608
EXPERTS = 16
SPLIT = 2
TOK_DEV = 128
CAP = 20
FFU = 2304
UNITS = 32
LAT = 512
IMAGES = 4
N_EP = 4


def levels(rng, extent, pieces, smallest, largest):
    level, own = 1.0, jax.random.fold_in(rng, 6)
    for position, shards_of in pieces:
        draws = jnp.exp(jax.random.uniform(jax.random.fold_in(own, position), (shards_of,), jnp.float32, smallest / len(pieces), largest / len(pieces)))
        level = level * jnp.repeat(draws, extent[position] // shards_of).reshape([-1 if axis == position else 1 for axis in range(len(extent))])
    return level


def shared_out(own_key, own, number, rows, number_of, top, bound, slope):
    order = jax.random.permutation(own_key, number_of)
    crowded, usual = shares(number_of, rows * top, bound, slope, True), shares(number_of, rows * top, bound, slope, False)
    places = jnp.arange(number_of)

    def named(lengths, rotation):
        used = int((lengths > 0).sum())
        fixed = max(1, used // 4)
        shifted = fixed + (places - fixed + rotation * (used - fixed)) % max(1, number_of - fixed)
        return jnp.zeros((number_of,), jnp.int32).at[order[jnp.where(places < fixed, places, shifted)]].set(jnp.asarray(lengths, jnp.int32))

    lengths = jnp.where(number % 4 == 0, named(crowded, number // 4), named(usual, number - number // 4 - 1))
    mixed = jax.random.permutation(jax.random.fold_in(own, 3), number_of)
    source_of, sink = mixed[0:number_of // 2 * 2:2], mixed[1:number_of // 2 * 2:2]
    margin = jnp.minimum(lengths[source_of] - 1, bound - lengths[sink]) // 2
    margin = jnp.where((source_of == order[0]) | (sink == order[0]) | (lengths[sink] == 0), 0, jnp.maximum(margin, 0))
    shifted = jax.random.randint(jax.random.fold_in(own, 4), (number_of // 2,), 0, 1 << 20) % (margin + 1)
    lengths = lengths.at[source_of].add(-shifted).at[sink].add(shifted)
    labels = jnp.searchsorted(jnp.cumsum(lengths), jnp.arange(rows * top), side="right").astype(jnp.int32)
    listing = labels.reshape(top, rows).T
    listing = listing[jax.random.permutation(jax.random.fold_in(own, 1), rows)]
    rotation = jax.random.randint(jax.random.fold_in(own, 2), (rows, 1), 0, top)
    return jnp.take_along_axis(listing, (jnp.arange(top)[None, :] + rotation) % top, axis=1)


def shares(count, total, reach, slope, full):
    portions = [(1 << 20) // math.isqrt(standing ** slope) + 1 for standing in range(1, count + 1)]
    largest = reach if full else min(reach, max(-(-total // count), total * portions[0] // sum(portions)))
    least = 1 if total - largest >= count - 1 else 0
    given, spare = [largest] + [least] * (count - 1), total - largest - least * (count - 1)
    while spare > 0:
        free = [i for i in range(1, count) if given[i] < largest] or [i for i in range(1, count) if given[i] < reach]
        mass, remaining = sum([portions[i] for i in free]), spare
        for i in free:
            more = min(reach - given[i], max(1, remaining * portions[i] // mass), spare)
            given[i] = given[i] + more
            spare = spare - more
    return np.array(given)


def normal_values(rng, extent, width, limit, shards=(), kind=jnp.bfloat16):
    factor_of = levels(rng, extent, shards, -0.22, 0.18) if shards else 1.0
    array = jax.random.normal(rng, extent, jnp.float32) * width * factor_of
    return jnp.minimum(jnp.maximum(array, -limit), limit).astype(kind)


def setup_inputs(seed: int = 0, part: int = 0) -> dict:
    streams_of = jax.random.split(jax.random.key(seed), 8)
    part_splits = jax.random.split(jax.random.fold_in(streams_of[7], part), 8)
    hidden_states = normal_values(part_splits[0], (IMAGES, LAT, D), 1.0, 6.0, ((0, 4), (1, 4)))
    expert_ids_keys = jax.random.split(jax.random.fold_in(part_splits[1], 1), IMAGES * LAT // TOK_DEV)
    expert_ids_turns = jax.random.permutation(jax.random.fold_in(part_splits[1], 3), IMAGES * LAT // TOK_DEV)
    expert_ids = jax.vmap(lambda own, number: shared_out(jax.random.fold_in(part_splits[1], 2), own, number, TOK_DEV, EXPERTS, 2, CAP, 1))(expert_ids_keys, expert_ids_turns).reshape((IMAGES, LAT, 2))
    modulation = normal_values(part_splits[2], (IMAGES, 3, D), 0.6, 4.0, ((0, 4),), jnp.float32)
    router_weight = normal_values(streams_of[3], (D, EXPERTS), D ** -0.5, 0.1875)
    w_in = normal_values(streams_of[4], (UNITS, D, FFU), D ** -0.5, 0.1875, ((0, 4), (1, 4)))
    b_in = normal_values(streams_of[5], (UNITS, FFU), 0.5, 3.0, ((0, 4),), jnp.float32)
    w_out = normal_values(streams_of[6], (UNITS, FFU, D), FF ** -0.5, 0.09375, ((0, 4), (1, 4)))
    return dict(hidden_states=hidden_states, expert_ids=expert_ids, modulation=modulation, router_weight=router_weight, w_in=w_in, b_in=b_in, w_out=w_out)


norm_eps = 1e-06

def modulate(tokens, shift, scale):
    values = tokens.astype(jnp.float32)
    center = lax.optimization_barrier(jnp.mean(values, axis=-1, keepdims=True))
    spread = lax.optimization_barrier(jnp.mean(jnp.square(values - center), axis=-1, keepdims=True))
    normal = (values - center) * lax.rsqrt(spread + norm_eps)
    return (normal * (1.0 + scale) + shift).astype(jnp.bfloat16)

def slot_index(block_ids):
    flat_ids = block_ids.reshape(-1)
    one_hot = (flat_ids[:, None] == jnp.arange(EXPERTS, dtype=jnp.int32)[None, :]).astype(jnp.int32)
    earlier = jnp.cumsum(one_hot, axis=0, dtype=jnp.int32) - one_hot
    slots = lax.optimization_barrier(jnp.sum(earlier * one_hot, axis=1, dtype=jnp.int32))
    return (flat_ids * CAP + slots).astype(jnp.int32).reshape(block_ids.shape)

def dispatch_rows(normed, flat_index):
    targets = jnp.arange(EXPERTS * CAP, dtype=jnp.int32)
    select = lax.optimization_barrier(jnp.sum((flat_index[None, :, :] == targets[:, None, None]).astype(jnp.int32), axis=2, dtype=jnp.int32))
    return jnp.dot(select.astype(jnp.bfloat16), normed, preferred_element_type=jnp.float32).astype(jnp.bfloat16)

def combine(tokens, normed, gate_row, router_weight, block_ids, flat_index, expert_out):
    logits = jnp.dot(normed, router_weight, preferred_element_type=jnp.float32)
    picked = jnp.take_along_axis(logits, block_ids, axis=1)
    gap = picked[:, 0:1] - picked[:, 1:2]
    first = jnp.take(expert_out, flat_index[:, 0], axis=0).astype(jnp.float32)
    second = jnp.take(expert_out, flat_index[:, 1], axis=0).astype(jnp.float32)
    branch = jax.nn.sigmoid(gap) * first + jax.nn.sigmoid(-gap) * second
    return (tokens.astype(jnp.float32) + gate_row[None, :] * branch).astype(jnp.bfloat16)

def reference(hidden_states, expert_ids, modulation, router_weight, w_in, b_in, w_out):
    blocks_x = hidden_states.reshape(IMAGES, N_EP, TOK_DEV, D)
    blocks_ids = expert_ids.reshape(IMAGES, N_EP, TOK_DEV, 2)
    normed = modulate(blocks_x, modulation[:, None, None, 0, :], modulation[:, None, None, 1, :])
    flat_index = jax.vmap(jax.vmap(slot_index))(blocks_ids)
    outgoing = jax.vmap(jax.vmap(dispatch_rows))(normed, flat_index)
    per_expert = outgoing.reshape(IMAGES, N_EP, EXPERTS, CAP, D).transpose(2, 0, 1, 3, 4)
    per_expert = per_expert.reshape(EXPERTS, IMAGES * N_EP * CAP, D)

    def unit_work(packed):
        unit, first_w, first_b, second_w = packed
        rows = lax.dynamic_index_in_dim(per_expert, unit // SPLIT, 0, keepdims=False)
        pre = jnp.dot(rows, first_w, preferred_element_type=jnp.float32) + first_b[None, :]
        hidden = jax.nn.gelu(pre, approximate=True).astype(jnp.bfloat16)
        return jnp.dot(hidden, second_w, preferred_element_type=jnp.float32).astype(jnp.bfloat16)
    piece_out = lax.map(unit_work, (jnp.arange(UNITS, dtype=jnp.int32), w_in, b_in, w_out))
    expert_out = lax.optimization_barrier(jnp.sum(piece_out.astype(jnp.float32).reshape(EXPERTS, SPLIT, IMAGES, N_EP, CAP, D), axis=1))
    expert_out = expert_out.astype(jnp.bfloat16)
    expert_out = expert_out.transpose(1, 2, 0, 3, 4).reshape(IMAGES, N_EP, EXPERTS * CAP, D)
    inner = jax.vmap(combine, in_axes=(0, 0, None, None, 0, 0, 0))
    outer = jax.vmap(inner, in_axes=(0, 0, 0, None, 0, 0, 0))
    result = outer(blocks_x, normed, modulation[:, 2, :], router_weight, blocks_ids, flat_index, expert_out)
    return result.reshape(IMAGES, LAT, D)
```

```python
import jax
import jax.numpy as jnp
from jax import lax
from jax.sharding import PartitionSpec as P

EXPERTS = 16
SPLIT = 2
CAP = 20


norm_eps = 1e-06


def swapped(block, axis, distance):
    count = lax.axis_size(axis)
    route = []
    for low in range(count):
        high = low | 1 << distance
        if high != low and high < count:
            route += [(low, high), (high, low)]
    return lax.ppermute(block, axis, route)


def modulate(tokens, shift, scale):
    values = tokens.astype(jnp.float32)
    center = jnp.mean(values, axis=-1, keepdims=True)
    spread = jnp.mean(jnp.square(values - center), axis=-1, keepdims=True)
    normal = (values - center) * lax.rsqrt(spread + norm_eps)
    return (normal * (1.0 + scale) + shift).astype(jnp.bfloat16)


def slot_index(block_ids):
    flat_ids = block_ids.reshape(-1)
    one_hot = (flat_ids[:, None] == jnp.arange(EXPERTS, dtype=jnp.int32)[None, :]).astype(jnp.int32)
    earlier = jnp.cumsum(one_hot, axis=0, dtype=jnp.int32) - one_hot
    slots = jnp.sum(earlier * one_hot, axis=1, dtype=jnp.int32)
    return (flat_ids * CAP + slots).reshape(block_ids.shape)


def dispatch_rows(normed, flat_index):
    targets = jnp.arange(EXPERTS * CAP, dtype=jnp.int32)
    select = jnp.sum(
        (flat_index[None, :, :] == targets[:, None, None]).astype(jnp.int32),
        axis=2,
        dtype=jnp.int32,
    )
    return jnp.dot(select.astype(jnp.bfloat16), normed, preferred_element_type=jnp.float32).astype(
        jnp.bfloat16
    )


def combine(tokens, normed, gate_row, router_weight, block_ids, flat_index, expert_out):
    logits = jnp.dot(normed, router_weight, preferred_element_type=jnp.float32)
    picked = jnp.take_along_axis(logits, block_ids, axis=1)
    gap = picked[:, 0:1] - picked[:, 1:2]
    first = jnp.take(expert_out, flat_index[:, 0], axis=0).astype(jnp.float32)
    second = jnp.take(expert_out, flat_index[:, 1], axis=0).astype(jnp.float32)
    branch = jax.nn.sigmoid(gap) * first + jax.nn.sigmoid(-gap) * second
    return (tokens.astype(jnp.float32) + gate_row[None, :] * branch).astype(jnp.bfloat16)


def expert_compute(incoming, w_in, b_in, w_out):
    columns = incoming
    pre_act = jnp.einsum(
        "urd,udf->urf",
        columns,
        lax.all_gather(w_in, "fs", axis=1, tiled=True),
        preferred_element_type=jnp.float32,
    )
    hidden = jax.nn.gelu(pre_act + b_in[:, None, :], approximate=True).astype(jnp.bfloat16)
    columns = hidden
    produced = jnp.einsum(
        "urf,ufd->urd",
        columns,
        lax.all_gather(w_out, "fs", axis=1, tiled=True),
        preferred_element_type=jnp.float32,
    )
    return produced.astype(jnp.bfloat16)


def local(hidden_states, expert_ids, modulation, router_weight, w_in, b_in, w_out):
    token_count = hidden_states.shape[1]
    width = hidden_states.shape[2]
    tokens = hidden_states.reshape(token_count, width)
    block_ids = expert_ids.reshape(token_count, 2)
    settings = modulation[0]
    normed = modulate(tokens, settings[0][None, :], settings[1][None, :])
    flat_index = slot_index(block_ids)
    outgoing = dispatch_rows(normed, flat_index)
    per_expert = outgoing.reshape(EXPERTS, CAP, width)
    members = lax.axis_size("ep")
    local_units = w_in.shape[0]
    paired = local_units == 1
    half_cap = CAP // 2
    if paired:
        sending = per_expert.reshape(members, half_cap, width)
    else:
        sending = per_expert
    received = lax.all_to_all(sending, "ep", split_axis=0, concat_axis=1, tiled=True)
    if paired:
        parity = lax.axis_index("ep") % 2
        partner = swapped(received, "ep", 0)
        own_blocks = received.reshape(members, half_cap, width)
        other_blocks = partner.reshape(members, half_cap, width)
        lower = jnp.where(parity == 0, own_blocks, other_blocks)
        upper = jnp.where(parity == 0, other_blocks, own_blocks)
        incoming = jnp.stack([lower, upper], axis=1).reshape(1, members * CAP, width)
    else:
        incoming = jnp.repeat(received, SPLIT, axis=0)
    produced = expert_compute(incoming, w_in, b_in, w_out)
    if paired:
        halves = produced.reshape(members, 2, half_cap, width)
        kept_rows = jnp.where(parity == 0, halves[:, 0], halves[:, 1])
        given_rows = jnp.where(parity == 0, halves[:, 1], halves[:, 0])
        partner_out = swapped(given_rows, "ep", 0)
        reply = (kept_rows.astype(jnp.float32) + partner_out.astype(jnp.float32)).astype(
            jnp.bfloat16
        )
    else:
        local_experts = local_units // SPLIT
        summed = jnp.sum(
            produced.astype(jnp.float32).reshape(local_experts, SPLIT, members, CAP, width), axis=1
        )
        reply = (
            summed.astype(jnp.bfloat16)
            .transpose(1, 0, 2, 3)
            .reshape(members, local_experts * CAP, width)
        )
    returned = lax.all_to_all(reply, "ep", split_axis=0, concat_axis=0, tiled=True)
    expert_out = returned.reshape(EXPERTS, CAP, width)
    result = combine(
        tokens,
        normed,
        settings[2],
        router_weight,
        block_ids,
        flat_index,
        expert_out.reshape(EXPERTS * CAP, width),
    )
    return result.reshape(1, token_count, width)


def fetched(block, axes, bit):
    count = lax.axis_size(axes)
    return lax.ppermute(block, axes, [(i, i ^ bit) for i in range(count)])


def one_hot(index, count):
    return (index[:, None] == jnp.arange(count, dtype=jnp.int32)[None, :]).astype(jnp.bfloat16)


def flat_slots(block_ids):
    flat_ids = block_ids.reshape(-1)
    pairs = flat_ids.shape[0]
    hot = one_hot(flat_ids, EXPERTS)
    order = jnp.arange(pairs, dtype=jnp.int32)
    before = (order[None, :] < order[:, None]).astype(jnp.bfloat16)
    earlier = jnp.dot(before, hot, preferred_element_type=jnp.float32)
    slots = jnp.sum(earlier * hot.astype(jnp.float32), axis=1).astype(jnp.int32)
    return (flat_ids * CAP + slots).reshape(block_ids.shape)


def mixed(tokens, normed, gate_row, router_weight, block_ids, picks, expert_out):
    logits = jnp.dot(normed, router_weight, preferred_element_type=jnp.float32)
    chosen = [
        jnp.sum(
            jnp.where(block_ids[:, k : k + 1] == jnp.arange(EXPERTS)[None, :], logits, 0.0),
            axis=1,
            keepdims=True,
        )
        for k in range(2)
    ]
    gap = chosen[0] - chosen[1]
    first = jnp.dot(picks[0], expert_out, preferred_element_type=jnp.float32)
    second = jnp.dot(picks[1], expert_out, preferred_element_type=jnp.float32)
    branch = jax.nn.sigmoid(gap) * first + jax.nn.sigmoid(-gap) * second
    return (tokens.astype(jnp.float32) + gate_row[None, :] * branch).astype(jnp.bfloat16)


def local_spread(hidden_states, expert_ids, modulation, router_weight, w_in, b_in, w_out):
    token_count = hidden_states.shape[1]
    width = hidden_states.shape[2]
    parts, members, shards = (lax.axis_size(a) for a in ("parts", "ep", "fs"))
    part, shard = lax.axis_index("parts"), lax.axis_index("fs")
    units = w_in.shape[0] // parts
    experts = units // SPLIT
    depth = w_in.shape[1]
    cols = w_in.shape[2] // shards

    mine = lax.dynamic_slice_in_dim(w_in, part * units, units, 0)
    strips = []
    for bit in range(shards):
        strip = lax.dynamic_slice_in_dim(mine, (shard ^ bit) * cols, cols, 2)
        strips.append(strip if bit == 0 else fetched(strip, "fs", bit))
    bias = lax.dynamic_slice(b_in, (part * units, shard * cols), (units, cols))
    second_w = lax.dynamic_slice_in_dim(w_out, part * units, units, 0)

    tokens = hidden_states.reshape(token_count, width)
    block_ids = expert_ids.reshape(token_count, 2)
    settings = modulation[0]
    normed = modulate(tokens, settings[0][None, :], settings[1][None, :])
    flat_index = flat_slots(block_ids)
    picks = [one_hot(flat_index[:, k], EXPERTS * CAP) for k in range(2)]
    outgoing = lax.dot_general(
        picks[0] + picks[1], normed, (((0,), (0,)), ((), ())), preferred_element_type=jnp.float32
    ).astype(jnp.bfloat16)
    sending = outgoing.reshape(members, parts, experts * CAP, width).transpose(1, 0, 2, 3)
    received = lax.all_to_all(
        sending.reshape(parts * members, experts * CAP, width),
        ("parts", "ep"),
        split_axis=0,
        concat_axis=0,
        tiled=True,
    )
    rows = parts * members * CAP
    own = (
        received.reshape(parts * members, experts, CAP, width)
        .transpose(1, 0, 2, 3)
        .reshape(experts, rows, width)
    )
    across = fetched(own, "fs", 2)
    beside = fetched(jnp.stack([own, across]), "fs", 1)
    images = [own, beside[0], across, beside[1]]
    incoming = jnp.concatenate(images, axis=1)

    incoming = jnp.repeat(incoming, SPLIT, axis=0)
    pre_act = bias[:, None, :]
    for bit in range(shards):
        piece = lax.dynamic_slice_in_dim(incoming, (shard ^ bit) * depth, depth, 2)
        pre_act = pre_act + jnp.einsum(
            "urd,udf->urf", piece, strips[bit], preferred_element_type=jnp.float32
        )
    hidden = jax.nn.gelu(pre_act, approximate=True).astype(jnp.bfloat16)
    produced = jnp.einsum("urf,ufd->urd", hidden, second_w, preferred_element_type=jnp.float32)
    total = jnp.sum(produced.reshape(experts, SPLIT, shards, rows, width), axis=1)
    given = fetched(total[:, 1::2].astype(jnp.bfloat16), "fs", 1)
    chip_sum = total[:, 0::2] + given.astype(jnp.float32)
    far = fetched(chip_sum[:, 1].astype(jnp.bfloat16), "fs", 2)
    summed = (chip_sum[:, 0] + far.astype(jnp.float32)).astype(jnp.bfloat16)
    reply = summed.reshape(experts, parts * members, CAP, width).transpose(1, 0, 2, 3)
    returned = lax.all_to_all(
        reply.reshape(parts * members, experts * CAP, width),
        ("parts", "ep"),
        split_axis=0,
        concat_axis=0,
        tiled=True,
    )
    expert_out = (
        returned.reshape(parts, members, experts * CAP, width)
        .transpose(1, 0, 2, 3)
        .reshape(EXPERTS * CAP, width)
    )
    result = mixed(
        tokens, normed, settings[2], router_weight, block_ids, picks, expert_out
    )
    return result.reshape(1, token_count, width)


def solution(mesh):
    sizes = mesh.shape
    spread = sizes["fs"] == 4 and EXPERTS % (sizes["ep"] * sizes["parts"]) == 0
    placed = (
        P(("parts", "fs"), "ep", None),
        P(("parts", "fs"), "ep", None),
        P(("parts", "fs"), None, None),
        P(),
        P("ep", "fs", None),
        P("ep", None),
        P("ep", "fs", None),
    )
    return jax.shard_map(
        local_spread if spread else local, mesh=mesh, in_specs=placed, out_specs=P(("parts", "fs"), "ep", None), check_vma=False
    )
```

```python
import functools

import jax
import jax.numpy as jnp
from jax import lax
from jax.experimental import pallas as pl
from jax.experimental.pallas import tpu as pltpu
from jax.sharding import PartitionSpec as P

EXPERTS = 16
SPLIT = 2
CAP = 20


norm_eps = 1e-06


def swapped(block, axis, distance):
    count = lax.axis_size(axis)
    route = []
    for low in range(count):
        high = low | 1 << distance
        if high != low and high < count:
            route += [(low, high), (high, low)]
    return lax.ppermute(block, axis, route)


def modulate(tokens, shift, scale):
    values = tokens.astype(jnp.float32)
    center = jnp.mean(values, axis=-1, keepdims=True)
    spread = jnp.mean(jnp.square(values - center), axis=-1, keepdims=True)
    normal = (values - center) * lax.rsqrt(spread + norm_eps)
    return (normal * (1.0 + scale) + shift).astype(jnp.bfloat16)


def slot_index(block_ids):
    flat_ids = block_ids.reshape(-1)
    one_hot = (flat_ids[:, None] == jnp.arange(EXPERTS, dtype=jnp.int32)[None, :]).astype(jnp.int32)
    earlier = jnp.cumsum(one_hot, axis=0, dtype=jnp.int32) - one_hot
    slots = jnp.sum(earlier * one_hot, axis=1, dtype=jnp.int32)
    return (flat_ids * CAP + slots).reshape(block_ids.shape)


def dispatch_rows(normed, flat_index):
    targets = jnp.arange(EXPERTS * CAP, dtype=jnp.int32)
    select = jnp.sum(
        (flat_index[None, :, :] == targets[:, None, None]).astype(jnp.int32),
        axis=2,
        dtype=jnp.int32,
    )
    return jnp.dot(select.astype(jnp.bfloat16), normed, preferred_element_type=jnp.float32).astype(
        jnp.bfloat16
    )


def combine(tokens, normed, gate_row, router_weight, block_ids, flat_index, expert_out):
    logits = jnp.dot(normed, router_weight, preferred_element_type=jnp.float32)
    picked = jnp.take_along_axis(logits, block_ids, axis=1)
    gap = picked[:, 0:1] - picked[:, 1:2]
    first = jnp.take(expert_out, flat_index[:, 0], axis=0).astype(jnp.float32)
    second = jnp.take(expert_out, flat_index[:, 1], axis=0).astype(jnp.float32)
    branch = jax.nn.sigmoid(gap) * first + jax.nn.sigmoid(-gap) * second
    return (tokens.astype(jnp.float32) + gate_row[None, :] * branch).astype(jnp.bfloat16)


def expert_compute(incoming, w_in, b_in, w_out):
    columns = incoming
    pre_act = jnp.einsum(
        "urd,udf->urf",
        columns,
        lax.all_gather(w_in, "fs", axis=1, tiled=True),
        preferred_element_type=jnp.float32,
    )
    hidden = jax.nn.gelu(pre_act + b_in[:, None, :], approximate=True).astype(jnp.bfloat16)
    columns = hidden
    produced = jnp.einsum(
        "urf,ufd->urd",
        columns,
        lax.all_gather(w_out, "fs", axis=1, tiled=True),
        preferred_element_type=jnp.float32,
    )
    return produced.astype(jnp.bfloat16)


def local(hidden_states, expert_ids, modulation, router_weight, w_in, b_in, w_out):
    token_count = hidden_states.shape[1]
    width = hidden_states.shape[2]
    tokens = hidden_states.reshape(token_count, width)
    block_ids = expert_ids.reshape(token_count, 2)
    settings = modulation[0]
    normed = modulate(tokens, settings[0][None, :], settings[1][None, :])
    flat_index = slot_index(block_ids)
    outgoing = dispatch_rows(normed, flat_index)
    per_expert = outgoing.reshape(EXPERTS, CAP, width)
    members = lax.axis_size("ep")
    local_units = w_in.shape[0]
    paired = local_units == 1
    half_cap = CAP // 2
    if paired:
        sending = per_expert.reshape(members, half_cap, width)
    else:
        sending = per_expert
    received = lax.all_to_all(sending, "ep", split_axis=0, concat_axis=1, tiled=True)
    if paired:
        parity = lax.axis_index("ep") % 2
        partner = swapped(received, "ep", 0)
        own_blocks = received.reshape(members, half_cap, width)
        other_blocks = partner.reshape(members, half_cap, width)
        lower = jnp.where(parity == 0, own_blocks, other_blocks)
        upper = jnp.where(parity == 0, other_blocks, own_blocks)
        incoming = jnp.stack([lower, upper], axis=1).reshape(1, members * CAP, width)
    else:
        incoming = jnp.repeat(received, SPLIT, axis=0)
    produced = expert_compute(incoming, w_in, b_in, w_out)
    if paired:
        halves = produced.reshape(members, 2, half_cap, width)
        kept_rows = jnp.where(parity == 0, halves[:, 0], halves[:, 1])
        given_rows = jnp.where(parity == 0, halves[:, 1], halves[:, 0])
        partner_out = swapped(given_rows, "ep", 0)
        reply = (kept_rows.astype(jnp.float32) + partner_out.astype(jnp.float32)).astype(
            jnp.bfloat16
        )
    else:
        local_experts = local_units // SPLIT
        summed = jnp.sum(
            produced.astype(jnp.float32).reshape(local_experts, SPLIT, members, CAP, width), axis=1
        )
        reply = (
            summed.astype(jnp.bfloat16)
            .transpose(1, 0, 2, 3)
            .reshape(members, local_experts * CAP, width)
        )
    returned = lax.all_to_all(reply, "ep", split_axis=0, concat_axis=0, tiled=True)
    expert_out = returned.reshape(EXPERTS, CAP, width)
    result = combine(
        tokens,
        normed,
        settings[2],
        router_weight,
        block_ids,
        flat_index,
        expert_out.reshape(EXPERTS * CAP, width),
    )
    return result.reshape(1, token_count, width)


def one_hot(index, count):
    return (index[:, None] == jnp.arange(count, dtype=jnp.int32)[None, :]).astype(jnp.bfloat16)


def flat_slots(block_ids):
    flat_ids = block_ids.reshape(-1)
    pairs = flat_ids.shape[0]
    hot = one_hot(flat_ids, EXPERTS)
    order = jnp.arange(pairs, dtype=jnp.int32)
    before = (order[None, :] < order[:, None]).astype(jnp.bfloat16)
    earlier = jnp.dot(before, hot, preferred_element_type=jnp.float32)
    slots = jnp.sum(earlier * hot.astype(jnp.float32), axis=1).astype(jnp.int32)
    return (flat_ids * CAP + slots).reshape(block_ids.shape)


def mixed(tokens, normed, gate_row, router_weight, block_ids, picks, expert_out):
    logits = jnp.dot(normed, router_weight, preferred_element_type=jnp.float32)
    chosen = [
        jnp.sum(
            jnp.where(block_ids[:, k : k + 1] == jnp.arange(EXPERTS)[None, :], logits, 0.0),
            axis=1,
            keepdims=True,
        )
        for k in range(2)
    ]
    gap = chosen[0] - chosen[1]
    first = jnp.dot(picks[0], expert_out, preferred_element_type=jnp.float32)
    second = jnp.dot(picks[1], expert_out, preferred_element_type=jnp.float32)
    branch = jax.nn.sigmoid(gap) * first + jax.nn.sigmoid(-gap) * second
    return (tokens.astype(jnp.float32) + gate_row[None, :] * branch).astype(jnp.bfloat16)


LANES = 128
PADDED = 64


def flip(index, bit):
    return index + bit * (1 - 2 * ((index // bit) % 2))


def flipped(index, distance, count):
    bit = 1
    while bit < count:
        if distance & bit:
            index = flip(index, bit)
        bit *= 2
    return index


def expert_kernel(
    sizes, send_ref, w_in_ref, bias_ref, w_out_ref, out_ref,
    got, rows_in, first_w, second_w, acc, r1_out, r1_in, r2_out, r2_in, r3_out,
    w_send, w_recv, second_sem, t1_send, t1_recv, t2_send, t2_recv,
    t3_send, t3_recv, t4_send, t4_recv,
    r1_send, r1_recv, r2_send, r2_recv, r3_send, r3_recv,
):
    parts, members, experts, units, cols, span, depth = sizes
    group = parts * members
    part, member, shard = (lax.axis_index(n) for n in ("parts", "ep", "fs"))

    def block_peer(d):
        return {
            "parts": flipped(part, d // members, parts),
            "ep": flipped(member, d % members, members),
            "fs": shard,
        }

    def shard_peer(bit):
        return {"parts": part, "ep": member, "fs": flipped(shard, bit, 4)}

    def remote(src, dst, send, recv, peer):
        return pltpu.make_async_remote_copy(
            src_ref=src, dst_ref=dst, send_sem=send, recv_sem=recv,
            device_id=peer, device_id_type=pl.DeviceIdType.MESH,
        )

    barrier = pltpu.get_barrier_semaphore()
    peers = [block_peer(d) for d in range(1, group)] + [shard_peer(b) for b in range(1, 4)]
    for peer in peers:
        pl.semaphore_signal(
            barrier, inc=1, device_id=peer, device_id_type=pl.DeviceIdType.MESH
        )
    pl.semaphore_wait(barrier, len(peers))

    def strip(u, bit):
        target = flipped(shard, bit, 4)
        start = pl.multiple_of((target * cols) // LANES * LANES, LANES)
        src = w_in_ref.at[part * units + u, :, pl.ds(start, span)]
        dst = first_w.at[u, pl.ds(pl.multiple_of(shard * depth, 32), depth), :]
        if bit == 0:
            return pltpu.make_async_copy(src, dst, w_recv.at[u, 0])
        return remote(src, dst, w_send.at[u, bit], w_recv.at[u, bit], shard_peer(bit))

    offset = (shard * cols) % LANES

    def second(u):
        place = pl.ds(pl.multiple_of(offset, PADDED), cols)
        return pltpu.make_async_copy(
            w_out_ref.at[part * units + u], second_w.at[u, place, :], second_sem.at[u]
        )

    def t1(d):
        if d == 0:
            return pltpu.make_async_copy(send_ref.at[0], got.at[0, 0], t1_recv.at[0])
        return remote(send_ref.at[d], got.at[0, d], t1_send.at[d], t1_recv.at[d], block_peer(d))

    def t2(d):
        return remote(got.at[0, d], got.at[2, d], t2_send.at[d], t2_recv.at[d], shard_peer(2))

    def t3(d):
        return remote(got.at[0, d], got.at[1, d], t3_send.at[d], t3_recv.at[d], shard_peer(1))

    def t4(d):
        return remote(got.at[2, d], got.at[3, d], t4_send.at[d], t4_recv.at[d], shard_peer(1))

    def r1(e):
        return remote(r1_out.at[e], r1_in.at[e], r1_send.at[e], r1_recv.at[e], shard_peer(1))

    def r2(e):
        return remote(r2_out.at[e], r2_in.at[e], r2_send.at[e], r2_recv.at[e], shard_peer(2))

    def r3(e, d):
        src, dst = r3_out.at[e, d], out_ref.at[d, e]
        if d == 0:
            return pltpu.make_async_copy(src, dst, r3_recv.at[e, 0])
        return remote(src, dst, r3_send.at[e, d], r3_recv.at[e, d], block_peer(d))

    for d in range(group):
        t1(d).start()
    early = units // experts
    for u in range(early):
        for bit in (2, 3, 1, 0):
            strip(u, bit).start()
    if span > cols:
        spare = (1 - offset // PADDED) * cols
        for u in range(units):
            second_w[u, pl.ds(pl.multiple_of(spare, PADDED), span - cols), :] = jnp.zeros(
                (span - cols, second_w.shape[2]), second_w.dtype
            )
    for u in range(units):
        second(u).start()

    def arrived(copy, d):
        if d == 0:
            copy.wait()
        else:
            copy.wait_recv()

    for d in range(group):
        arrived(t1(d), d)
        t2(d).start()
        t3(d).start()
    for u in range(early, units):
        for bit in (2, 3, 1, 0):
            strip(u, bit).start()
    for d in range(group):
        t2(d).wait_recv()
        t4(d).start()

    half = group * CAP
    batch = 4 if group % 4 == 0 else 1

    def arrange(images, side):
        for place, image in enumerate(images):
            for low in range(0, group, batch):
                chunks = [got[image, low + i] for i in range(batch)]
                for e in range(experts):
                    rows_in[e, side, pl.ds(place * half + low * CAP, batch * CAP), :] = (
                        jnp.concatenate([c[e * CAP : (e + 1) * CAP] for c in chunks], axis=0)
                    )

    arrange((0, 2), 0)
    for d in range(group):
        t3(d).wait_recv()
        t4(d).wait_recv()
    arrange((1, 3), 1)

    def reply(e):
        r2(e).wait_recv()
        total = acc_keep(e) + r2_in[e].astype(jnp.float32)
        total = total.astype(jnp.bfloat16)
        for d in range(group):
            r3_out[e, d] = total[d * CAP : (d + 1) * CAP]
        for d in range(group):
            r3(e, d).start()

    def acc_keep(e):
        return acc[e, 0, 0:half, :]

    for e in range(experts):
        for p in range(SPLIT):
            u = e * SPLIT + p
            strip(u, 0).wait()
            for bit in (1, 2, 3):
                strip(u, bit).wait_recv()
            second(u).wait()
            for side in (1, 0):
                pre = jnp.dot(
                    rows_in[e, side], first_w[u], preferred_element_type=jnp.float32
                )
                hidden = jax.nn.gelu(pre + bias_ref[u], approximate=True).astype(jnp.bfloat16)
                made = jnp.dot(hidden, second_w[u], preferred_element_type=jnp.float32)
                if p > 0:
                    made = made + acc[e, side]
                if p == SPLIT - 1 and side == 1:
                    r1_out[e] = made.astype(jnp.bfloat16)
                    r1(e).start()
                else:
                    acc[e, side] = made
            if p == 0 and e > 0:
                reply(e - 1)
        r1(e).wait_recv()
        chip = acc[e, 0] + r1_in[e].astype(jnp.float32)
        r2_out[e] = chip[half:].astype(jnp.bfloat16)
        r2(e).start()
        acc[e, 0] = chip
    reply(experts - 1)

    for e in range(experts):
        for d in range(group):
            arrived(r3(e, d), d)
            if d > 0:
                r3(e, d).wait_send()
        r1(e).wait_send()
        r2(e).wait_send()
    for u in range(units):
        for bit in (1, 2, 3):
            strip(u, bit).wait_send()
    for d in range(group):
        if d > 0:
            t1(d).wait_send()
        t2(d).wait_send()
        t3(d).wait_send()
        t4(d).wait_send()


def local_spread(hidden_states, expert_ids, modulation, router_weight, w_in, b_in, w_out):
    token_count = hidden_states.shape[1]
    width = hidden_states.shape[2]
    parts, members, shards = (lax.axis_size(a) for a in ("parts", "ep", "fs"))
    part, member, shard = (lax.axis_index(a) for a in ("parts", "ep", "fs"))
    group = parts * members
    units = w_in.shape[0] // parts
    experts = units // SPLIT
    depth = w_in.shape[1]
    cols = w_in.shape[2] // shards
    span = cols + cols % LANES

    start = shard * cols // LANES * LANES
    bias = lax.dynamic_slice(b_in, (part * units, start), (units, span))[:, None, :]

    tokens = hidden_states.reshape(token_count, width)
    block_ids = expert_ids.reshape(token_count, 2)
    settings = modulation[0]
    normed = modulate(tokens, settings[0][None, :], settings[1][None, :])
    slots = flat_slots(block_ids) - block_ids * CAP
    holder_member = block_ids // (parts * experts)
    holder_part = block_ids // experts % parts
    distance = (holder_part * members + holder_member) ^ (part * members + member)
    place = (distance * experts + block_ids % experts) * CAP + slots
    picks = [one_hot(place[:, k], EXPERTS * CAP) for k in range(2)]
    sending = lax.dot_general(
        picks[0] + picks[1], normed, (((0,), (0,)), ((), ())), preferred_element_type=jnp.float32
    ).astype(jnp.bfloat16)

    rows = 2 * group * CAP
    bf16, dma = jnp.bfloat16, pltpu.SemaphoreType.DMA
    hbm, vmem = pl.BlockSpec(memory_space=pl.ANY), pl.BlockSpec(memory_space=pltpu.VMEM)
    sizes = (parts, members, experts, units, cols, span, depth)
    returned = pl.pallas_call(
        functools.partial(expert_kernel, sizes),
        out_shape=jax.ShapeDtypeStruct((group, experts, CAP, width), bf16),
        in_specs=[hbm, hbm, vmem, hbm],
        out_specs=hbm,
        scratch_shapes=[
            pltpu.VMEM((shards, group, experts * CAP, width), bf16),
            pltpu.VMEM((experts, 2, rows, width), bf16),
            pltpu.VMEM((units, width, span), bf16),
            pltpu.VMEM((units, span, width), bf16),
            pltpu.VMEM((experts, 2, rows, width), jnp.float32),
            pltpu.VMEM((experts, rows, width), bf16),
            pltpu.VMEM((experts, rows, width), bf16),
            pltpu.VMEM((experts, rows // 2, width), bf16),
            pltpu.VMEM((experts, rows // 2, width), bf16),
            pltpu.VMEM((experts, group, CAP, width), bf16),
            dma((units, 4)), dma((units, 4)), dma((units,)),
        ]
        + [dma((group,))] * 8
        + [dma((experts,))] * 4
        + [dma((experts, group))] * 2,
        compiler_params=pltpu.CompilerParams(
            collective_id=0, has_side_effects=True, vmem_limit_bytes=60 * 1024 * 1024
        ),
    )(sending.reshape(group, experts * CAP, width), w_in, bias, w_out)

    expert_out = returned.reshape(EXPERTS * CAP, width)
    result = mixed(
        tokens, normed, settings[2], router_weight, block_ids, picks, expert_out
    )
    return result.reshape(1, token_count, width)


def solution(mesh):
    sizes = mesh.shape
    group = sizes["ep"] * sizes["parts"]
    spread = sizes["fs"] == 4 and EXPERTS % group == 0
    placed = (
        P(("parts", "fs"), "ep", None),
        P(("parts", "fs"), "ep", None),
        P(("parts", "fs"), None, None),
        P(),
        P("ep", "fs", None),
        P("ep", None),
        P("ep", "fs", None),
    )
    return jax.shard_map(
        local_spread if spread else local, mesh=mesh, in_specs=placed, out_specs=P(("parts", "fs"), "ep", None), check_vma=False
    )
```

```python
import functools

import jax
import jax.numpy as jnp
from jax import lax
from jax.experimental import pallas as pl
from jax.experimental.pallas import tpu as pltpu
from jax.sharding import PartitionSpec as P

EXPERTS = 16
SPLIT = 2
CAP = 20


norm_eps = 1e-06


def swapped(block, axis, distance):
    count = lax.axis_size(axis)
    route = []
    for low in range(count):
        high = low | 1 << distance
        if high != low and high < count:
            route += [(low, high), (high, low)]
    return lax.ppermute(block, axis, route)


def modulate(tokens, shift, scale):
    values = tokens.astype(jnp.float32)
    center = jnp.mean(values, axis=-1, keepdims=True)
    spread = jnp.mean(jnp.square(values - center), axis=-1, keepdims=True)
    normal = (values - center) * lax.rsqrt(spread + norm_eps)
    return (normal * (1.0 + scale) + shift).astype(jnp.bfloat16)


def slot_index(block_ids):
    flat_ids = block_ids.reshape(-1)
    one_hot = (flat_ids[:, None] == jnp.arange(EXPERTS, dtype=jnp.int32)[None, :]).astype(jnp.int32)
    earlier = jnp.cumsum(one_hot, axis=0, dtype=jnp.int32) - one_hot
    slots = jnp.sum(earlier * one_hot, axis=1, dtype=jnp.int32)
    return (flat_ids * CAP + slots).reshape(block_ids.shape)


def dispatch_rows(normed, flat_index):
    targets = jnp.arange(EXPERTS * CAP, dtype=jnp.int32)
    select = jnp.sum(
        (flat_index[None, :, :] == targets[:, None, None]).astype(jnp.int32),
        axis=2,
        dtype=jnp.int32,
    )
    return jnp.dot(select.astype(jnp.bfloat16), normed, preferred_element_type=jnp.float32).astype(
        jnp.bfloat16
    )


def combine(tokens, normed, gate_row, router_weight, block_ids, flat_index, expert_out):
    logits = jnp.dot(normed, router_weight, preferred_element_type=jnp.float32)
    picked = jnp.take_along_axis(logits, block_ids, axis=1)
    gap = picked[:, 0:1] - picked[:, 1:2]
    first = jnp.take(expert_out, flat_index[:, 0], axis=0).astype(jnp.float32)
    second = jnp.take(expert_out, flat_index[:, 1], axis=0).astype(jnp.float32)
    branch = jax.nn.sigmoid(gap) * first + jax.nn.sigmoid(-gap) * second
    return (tokens.astype(jnp.float32) + gate_row[None, :] * branch).astype(jnp.bfloat16)


def expert_compute(incoming, w_in, b_in, w_out):
    columns = incoming
    pre_act = jnp.einsum(
        "urd,udf->urf",
        columns,
        lax.all_gather(w_in, "fs", axis=1, tiled=True),
        preferred_element_type=jnp.float32,
    )
    hidden = jax.nn.gelu(pre_act + b_in[:, None, :], approximate=True).astype(jnp.bfloat16)
    columns = hidden
    produced = jnp.einsum(
        "urf,ufd->urd",
        columns,
        lax.all_gather(w_out, "fs", axis=1, tiled=True),
        preferred_element_type=jnp.float32,
    )
    return produced.astype(jnp.bfloat16)


def local(hidden_states, expert_ids, modulation, router_weight, w_in, b_in, w_out):
    token_count = hidden_states.shape[1]
    width = hidden_states.shape[2]
    tokens = hidden_states.reshape(token_count, width)
    block_ids = expert_ids.reshape(token_count, 2)
    settings = modulation[0]
    normed = modulate(tokens, settings[0][None, :], settings[1][None, :])
    flat_index = slot_index(block_ids)
    outgoing = dispatch_rows(normed, flat_index)
    per_expert = outgoing.reshape(EXPERTS, CAP, width)
    members = lax.axis_size("ep")
    local_units = w_in.shape[0]
    paired = local_units == 1
    half_cap = CAP // 2
    if paired:
        sending = per_expert.reshape(members, half_cap, width)
    else:
        sending = per_expert
    received = lax.all_to_all(sending, "ep", split_axis=0, concat_axis=1, tiled=True)
    if paired:
        parity = lax.axis_index("ep") % 2
        partner = swapped(received, "ep", 0)
        own_blocks = received.reshape(members, half_cap, width)
        other_blocks = partner.reshape(members, half_cap, width)
        lower = jnp.where(parity == 0, own_blocks, other_blocks)
        upper = jnp.where(parity == 0, other_blocks, own_blocks)
        incoming = jnp.stack([lower, upper], axis=1).reshape(1, members * CAP, width)
    else:
        incoming = jnp.repeat(received, SPLIT, axis=0)
    produced = expert_compute(incoming, w_in, b_in, w_out)
    if paired:
        halves = produced.reshape(members, 2, half_cap, width)
        kept_rows = jnp.where(parity == 0, halves[:, 0], halves[:, 1])
        given_rows = jnp.where(parity == 0, halves[:, 1], halves[:, 0])
        partner_out = swapped(given_rows, "ep", 0)
        reply = (kept_rows.astype(jnp.float32) + partner_out.astype(jnp.float32)).astype(
            jnp.bfloat16
        )
    else:
        local_experts = local_units // SPLIT
        summed = jnp.sum(
            produced.astype(jnp.float32).reshape(local_experts, SPLIT, members, CAP, width), axis=1
        )
        reply = (
            summed.astype(jnp.bfloat16)
            .transpose(1, 0, 2, 3)
            .reshape(members, local_experts * CAP, width)
        )
    returned = lax.all_to_all(reply, "ep", split_axis=0, concat_axis=0, tiled=True)
    expert_out = returned.reshape(EXPERTS, CAP, width)
    result = combine(
        tokens,
        normed,
        settings[2],
        router_weight,
        block_ids,
        flat_index,
        expert_out.reshape(EXPERTS * CAP, width),
    )
    return result.reshape(1, token_count, width)


LANES = 128
HALF_LANES = 64


def flip(index, bit):
    return index + bit * (1 - 2 * ((index // bit) % 2))


def flipped(index, distance, count):
    bit = 1
    while bit < count:
        if distance & bit:
            index = flip(index, bit)
        bit *= 2
    return index


def expert_kernel(
    sizes, hidden_ref, ids_ref, settings_ref, router_ref, w_in_ref, bias_ref, w_out_ref, out_ref,
    send, got, rows_in, first_w, second_w, acc, r1_out, r1_in, r2_out, r2_in, r3_out, back,
    w_send, w_recv, second_sem, edge_send, edge_recv,
    t1_send, t1_recv, t2_send, t2_recv, t3_send, t3_recv, t4_send, t4_recv,
    r1_send, r1_recv, r2_send, r2_recv, r3_send, r3_recv,
):
    parts, members, experts, units, cols, span, depth, pieces = sizes
    group = parts * members
    part, member, shard = (lax.axis_index(n) for n in ("parts", "ep", "fs"))

    def block_peer(d):
        return {
            "parts": flipped(part, d // members, parts),
            "ep": flipped(member, d % members, members),
            "fs": shard,
        }

    def shard_peer(bit):
        return {"parts": part, "ep": member, "fs": flipped(shard, bit, 4)}

    def remote(src, dst, send, recv, peer):
        return pltpu.make_async_remote_copy(
            src_ref=src, dst_ref=dst, send_sem=send, recv_sem=recv,
            device_id=peer, device_id_type=pl.DeviceIdType.MESH,
        )

    barrier = pltpu.get_barrier_semaphore()
    peers = [block_peer(d) for d in range(1, group)] + [shard_peer(b) for b in range(1, 4)]
    for peer in peers:
        pl.semaphore_signal(
            barrier, inc=1, device_id=peer, device_id_type=pl.DeviceIdType.MESH
        )
    pl.semaphore_wait(barrier, len(peers))

    even = shard % 2 == 0
    rest = span - LANES

    def strip(u, bit, wide):
        target = flipped(shard, bit, 4)
        start = target // 2 * (2 * cols) + (0 if wide else span)
        start = pl.multiple_of(start, LANES)
        src = w_in_ref.at[part * units + u, :, pl.ds(start, span if wide else rest)]
        rows = pl.ds(pl.multiple_of(shard * depth, 32), depth)
        dst = first_w.at[u, rows, :] if wide else first_w.at[u, rows, pl.ds(LANES, rest)]
        if bit == 0:
            return pltpu.make_async_copy(src, dst, w_recv.at[u, 0])
        return remote(src, dst, w_send.at[u, bit], w_recv.at[u, bit], shard_peer(bit))

    def strips_start(u):
        @pl.when(even)
        def _():
            for bit in (2, 3, 1, 0):
                strip(u, bit, bit % 2 == 0).start()

        @pl.when(shard % 2 == 1)
        def _():
            for bit in (2, 3, 1, 0):
                strip(u, bit, bit % 2 == 1).start()

    def edge(u):
        return remote(
            w_out_ref.at[part * units + u, pl.ds(0, HALF_LANES), :],
            second_w.at[u, pl.ds(cols, HALF_LANES), :],
            edge_send.at[u], edge_recv.at[u], shard_peer(1),
        )

    def second_even(u):
        return pltpu.make_async_copy(
            w_out_ref.at[part * units + u], second_w.at[u, pl.ds(0, cols), :], second_sem.at[u]
        )

    def second_odd(u):
        return pltpu.make_async_copy(
            w_out_ref.at[part * units + u, pl.ds(HALF_LANES, rest), :],
            second_w.at[u, pl.ds(LANES, rest), :],
            second_sem.at[u],
        )

    def weights_wait(u):
        @pl.when(even)
        def _():
            strip(u, 0, True).wait()
            for bit in (1, 2, 3):
                strip(u, bit, True).wait_recv()
            second_even(u).wait()
            edge(u).wait_recv()

        @pl.when(shard % 2 == 1)
        def _():
            strip(u, 0, False).wait()
            for bit in (1, 2, 3):
                strip(u, bit, False).wait_recv()
            second_odd(u).wait()

    def t1(d):
        if d == 0:
            return pltpu.make_async_copy(send.at[0], got.at[0, 0], t1_recv.at[0])
        return remote(send.at[d], got.at[0, d], t1_send.at[d], t1_recv.at[d], block_peer(d))

    def t2(d):
        return remote(got.at[0, d], got.at[2, d], t2_send.at[d], t2_recv.at[d], shard_peer(2))

    def t3(d):
        return remote(got.at[0, d], got.at[1, d], t3_send.at[d], t3_recv.at[d], shard_peer(1))

    def t4(d):
        return remote(got.at[2, d], got.at[3, d], t4_send.at[d], t4_recv.at[d], shard_peer(1))

    def r1(e):
        return remote(r1_out.at[e], r1_in.at[e], r1_send.at[e], r1_recv.at[e], shard_peer(1))

    def r2(e, i):
        return remote(
            r2_out.at[e, i], r2_in.at[e, i], r2_send.at[e, i], r2_recv.at[e, i], shard_peer(2)
        )

    def r3(e, d):
        src, dst = r3_out.at[e, d], back.at[e, d]
        if d == 0:
            return pltpu.make_async_copy(src, dst, r3_recv.at[e, 0])
        return remote(src, dst, r3_send.at[e, d], r3_recv.at[e, d], block_peer(d))

    early = units // experts
    for u in range(early):
        strips_start(u)

    @pl.when(even)
    def _():
        for u in range(units):
            second_even(u).start()

    @pl.when(shard % 2 == 1)
    def _():
        for u in range(units):
            edge(u).start()
            second_odd(u).start()
            first_w[u, :, 0:LANES] = jnp.zeros((first_w.shape[1], LANES), first_w.dtype)
            second_w[u, 0:LANES, :] = jnp.zeros((LANES, second_w.shape[2]), second_w.dtype)

    tokens = hidden_ref[...]
    count = tokens.shape[0]
    normed = modulate(tokens, settings_ref[0:1, :], settings_ref[1:2, :])
    f32, bf16 = jnp.float32, jnp.bfloat16
    expert_rows = lax.broadcasted_iota(jnp.int32, (EXPERTS, count), 0)
    ids = [ids_ref[k : k + 1, :] for k in range(2)]
    hot = [(expert_rows == ids[k]).astype(f32) for k in range(2)]
    before = (
        lax.broadcasted_iota(jnp.int32, (count, count), 0)
        < lax.broadcasted_iota(jnp.int32, (count, count), 1)
    ).astype(f32)
    earlier = jnp.dot(
        (hot[0] + hot[1]).astype(bf16), before.astype(bf16), preferred_element_type=f32
    )
    slots = [jnp.sum(earlier * hot[k], axis=0, keepdims=True).astype(jnp.int32) for k in range(2)]
    own_index = part * members + member
    holder = [
        ((i // experts % parts) * members + i // (parts * experts)) ^ own_index for i in ids
    ]
    at_holder = [i % experts for i in ids]
    total_rows = group * experts * CAP
    place_rows = lax.broadcasted_iota(jnp.int32, (total_rows, count), 0)
    select = sum(
        (place_rows == (holder[k] * experts + at_holder[k]) * CAP + slots[k]).astype(f32)
        for k in range(2)
    )
    outgoing = jnp.dot(select.astype(bf16), normed, preferred_element_type=f32).astype(bf16)
    for d in range(group):
        send[d] = outgoing[d * experts * CAP : (d + 1) * experts * CAP]
    for d in range(group):
        t1(d).start()

    logits = lax.dot_general(
        router_ref[...], normed, (((1,), (1,)), ((), ())), preferred_element_type=f32
    )
    chosen = [jnp.sum(logits * hot[k], axis=0, keepdims=True) for k in range(2)]
    gap = jnp.broadcast_to(chosen[0] - chosen[1], (count, count)).T[:, 0:1]
    mix = [jax.nn.sigmoid(gap), jax.nn.sigmoid(-gap)]
    places = [(at_holder[k] * group + holder[k]) * CAP + slots[k] for k in range(2)]

    def arrived(copy, d):
        if d == 0:
            copy.wait()
        else:
            copy.wait_recv()

    for d in range(group):
        arrived(t1(d), d)
        t2(d).start()
        t3(d).start()
    for u in range(early, units):
        strips_start(u)
    for d in range(group):
        t2(d).wait_recv()
        t4(d).start()

    half = group * CAP
    batch = 4 if group % 4 == 0 else 1

    def arrange(images, side):
        for place, image in enumerate(images):
            for low in range(0, group, batch):
                chunks = [got[image, low + i] for i in range(batch)]
                for e in range(experts):
                    rows_in[e, side, pl.ds(place * half + low * CAP, batch * CAP), :] = (
                        jnp.concatenate([c[e * CAP : (e + 1) * CAP] for c in chunks], axis=0)
                    )

    arrange((0, 2), 0)
    for d in range(group):
        t3(d).wait_recv()
        t4(d).wait_recv()
    arrange((1, 3), 1)

    piece = half // pieces
    in_piece = group // pieces

    def reply(e):
        for i in range(pieces):
            r2(e, i).wait_recv()
            total = acc[e, 0, i * piece : (i + 1) * piece, :] + r2_in[e, i].astype(f32)
            total = total.astype(bf16)
            for j in range(in_piece):
                r3_out[e, i * in_piece + j] = total[j * CAP : (j + 1) * CAP]
            for j in range(in_piece):
                r3(e, i * in_piece + j).start()

    def picked(e):
        for d in range(group):
            arrived(r3(e, d), d)
        rows = jnp.concatenate([back[e, d] for d in range(group)], axis=0)
        columns = lax.broadcasted_iota(jnp.int32, (half, count), 0) + e * half
        branch = 0.0
        for k in range(2):
            pick = (columns == places[k]).astype(f32).astype(bf16)
            branch = branch + mix[k] * lax.dot_general(
                pick, rows, (((0,), (0,)), ((), ())), preferred_element_type=f32
            )
        return branch

    for e in range(experts):
        for p in range(SPLIT):
            u = e * SPLIT + p
            weights_wait(u)
            start = pl.multiple_of(shard // 2 * (2 * cols) + shard % 2 * (span - LANES), LANES)
            bias = bias_ref[pl.ds(part * units + u, 1), pl.ds(start, span)]
            for side in (1, 0):
                pre = jnp.dot(
                    rows_in[e, side], first_w[u], preferred_element_type=jnp.float32
                )
                hidden = jax.nn.gelu(pre + bias, approximate=True).astype(jnp.bfloat16)
                made = jnp.dot(hidden, second_w[u], preferred_element_type=jnp.float32)
                if p > 0:
                    made = made + acc[e, side]
                if p == SPLIT - 1 and side == 1:
                    r1_out[e] = made.astype(jnp.bfloat16)
                    r1(e).start()
                else:
                    acc[e, side] = made
            if p == 0 and e > 0:
                reply(e - 1)
        r1(e).wait_recv()
        chip = acc[e, 0] + r1_in[e].astype(jnp.float32)
        for i in range(pieces):
            r2_out[e, i] = chip[half + i * piece : half + (i + 1) * piece].astype(bf16)
        for i in range(pieces):
            r2(e, i).start()
        acc[e, 0] = chip
    reply(experts - 1)

    branch = sum(picked(e) for e in range(experts))
    out_ref[...] = (tokens.astype(f32) + settings_ref[2:3, :] * branch).astype(bf16)

    for e in range(experts):
        for d in range(1, group):
            r3(e, d).wait_send()
        r1(e).wait_send()
        for i in range(pieces):
            r2(e, i).wait_send()

    @pl.when(even)
    def _():
        for u in range(units):
            for bit in (1, 2, 3):
                strip(u, bit, bit % 2 == 0).wait_send()

    @pl.when(shard % 2 == 1)
    def _():
        for u in range(units):
            edge(u).wait_send()
            for bit in (1, 2, 3):
                strip(u, bit, bit % 2 == 1).wait_send()

    for d in range(group):
        if d > 0:
            t1(d).wait_send()
        t2(d).wait_send()
        t3(d).wait_send()
        t4(d).wait_send()


def local_spread(hidden_states, expert_ids, modulation, router_weight, w_in, b_in, w_out):
    token_count = hidden_states.shape[1]
    width = hidden_states.shape[2]
    parts, members, shards = (lax.axis_size(a) for a in ("parts", "ep", "fs"))
    group = parts * members
    units = w_in.shape[0] // parts
    experts = units // SPLIT
    depth = w_in.shape[1]
    cols = w_in.shape[2] // shards
    span = cols + cols % LANES
    pieces = 4 if group % 4 == 0 else 1

    rows = 2 * group * CAP
    bf16, dma = jnp.bfloat16, pltpu.SemaphoreType.DMA
    hbm, vmem = pl.BlockSpec(memory_space=pl.ANY), pl.BlockSpec(memory_space=pltpu.VMEM)
    sizes = (parts, members, experts, units, cols, span, depth, pieces)
    result = pl.pallas_call(
        functools.partial(expert_kernel, sizes),
        out_shape=jax.ShapeDtypeStruct((token_count, width), bf16),
        in_specs=[vmem, vmem, vmem, vmem, hbm, vmem, hbm],
        out_specs=vmem,
        scratch_shapes=[
            pltpu.VMEM((group, experts * CAP, width), bf16),
            pltpu.VMEM((shards, group, experts * CAP, width), bf16),
            pltpu.VMEM((experts, 2, rows, width), bf16),
            pltpu.VMEM((units, width, span), bf16),
            pltpu.VMEM((units, span, width), bf16),
            pltpu.VMEM((experts, 2, rows, width), jnp.float32),
            pltpu.VMEM((experts, rows, width), bf16),
            pltpu.VMEM((experts, rows, width), bf16),
            pltpu.VMEM((experts, pieces, rows // 2 // pieces, width), bf16),
            pltpu.VMEM((experts, pieces, rows // 2 // pieces, width), bf16),
            pltpu.VMEM((experts, group, CAP, width), bf16),
            pltpu.VMEM((experts, group, CAP, width), bf16),
            dma((units, 4)), dma((units, 4)), dma((units,)),
            dma((units,)), dma((units,)),
        ]
        + [dma((group,))] * 8
        + [dma((experts,))] * 2
        + [dma((experts, pieces))] * 2
        + [dma((experts, group))] * 2,
        compiler_params=pltpu.CompilerParams(
            collective_id=0, has_side_effects=True, vmem_limit_bytes=60 * 1024 * 1024
        ),
    )(
        hidden_states.reshape(token_count, width),
        expert_ids.reshape(token_count, 2).T,
        modulation[0],
        router_weight.T,
        w_in,
        b_in,
        w_out,
    )
    return result.reshape(1, token_count, width)


def solution(mesh):
    sizes = mesh.shape
    group = sizes["ep"] * sizes["parts"]
    spread = sizes["fs"] == 4 and EXPERTS % group == 0 and sizes["parts"] == 2
    placed = (
        P(("parts", "fs"), "ep", None),
        P(("parts", "fs"), "ep", None),
        P(("parts", "fs"), None, None),
        P(),
        P("ep", "fs", None),
        P("ep", None),
        P("ep", "fs", None),
    )
    return jax.shard_map(
        local_spread if spread else local, mesh=mesh, in_specs=placed, out_specs=P(("parts", "fs"), "ep", None), check_vma=False
    )
```

```python
import functools

import jax
import jax.numpy as jnp
from jax import lax
from jax.experimental import pallas as pl
from jax.experimental.pallas import tpu as pltpu
from jax.sharding import PartitionSpec as P

EXPERTS = 16
SPLIT = 2
CAP = 20


norm_eps = 1e-06


def swapped(block, axis, distance):
    count = lax.axis_size(axis)
    route = []
    for low in range(count):
        high = low | 1 << distance
        if high != low and high < count:
            route += [(low, high), (high, low)]
    return lax.ppermute(block, axis, route)


def modulate(tokens, shift, scale):
    values = tokens.astype(jnp.float32)
    center = jnp.mean(values, axis=-1, keepdims=True)
    spread = jnp.mean(jnp.square(values - center), axis=-1, keepdims=True)
    normal = (values - center) * lax.rsqrt(spread + norm_eps)
    return (normal * (1.0 + scale) + shift).astype(jnp.bfloat16)


def slot_index(block_ids):
    flat_ids = block_ids.reshape(-1)
    one_hot = (flat_ids[:, None] == jnp.arange(EXPERTS, dtype=jnp.int32)[None, :]).astype(jnp.int32)
    earlier = jnp.cumsum(one_hot, axis=0, dtype=jnp.int32) - one_hot
    slots = jnp.sum(earlier * one_hot, axis=1, dtype=jnp.int32)
    return (flat_ids * CAP + slots).reshape(block_ids.shape)


def dispatch_rows(normed, flat_index):
    targets = jnp.arange(EXPERTS * CAP, dtype=jnp.int32)
    select = jnp.sum(
        (flat_index[None, :, :] == targets[:, None, None]).astype(jnp.int32),
        axis=2,
        dtype=jnp.int32,
    )
    return jnp.dot(select.astype(jnp.bfloat16), normed, preferred_element_type=jnp.float32).astype(
        jnp.bfloat16
    )


def combine(tokens, normed, gate_row, router_weight, block_ids, flat_index, expert_out):
    logits = jnp.dot(normed, router_weight, preferred_element_type=jnp.float32)
    picked = jnp.take_along_axis(logits, block_ids, axis=1)
    gap = picked[:, 0:1] - picked[:, 1:2]
    first = jnp.take(expert_out, flat_index[:, 0], axis=0).astype(jnp.float32)
    second = jnp.take(expert_out, flat_index[:, 1], axis=0).astype(jnp.float32)
    branch = jax.nn.sigmoid(gap) * first + jax.nn.sigmoid(-gap) * second
    return (tokens.astype(jnp.float32) + gate_row[None, :] * branch).astype(jnp.bfloat16)


def expert_compute(incoming, w_in, b_in, w_out):
    columns = incoming
    pre_act = jnp.einsum(
        "urd,udf->urf",
        columns,
        lax.all_gather(w_in, "fs", axis=1, tiled=True),
        preferred_element_type=jnp.float32,
    )
    hidden = jax.nn.gelu(pre_act + b_in[:, None, :], approximate=True).astype(jnp.bfloat16)
    columns = hidden
    produced = jnp.einsum(
        "urf,ufd->urd",
        columns,
        lax.all_gather(w_out, "fs", axis=1, tiled=True),
        preferred_element_type=jnp.float32,
    )
    return produced.astype(jnp.bfloat16)


def local(hidden_states, expert_ids, modulation, router_weight, w_in, b_in, w_out):
    token_count = hidden_states.shape[1]
    width = hidden_states.shape[2]
    tokens = hidden_states.reshape(token_count, width)
    block_ids = expert_ids.reshape(token_count, 2)
    settings = modulation[0]
    normed = modulate(tokens, settings[0][None, :], settings[1][None, :])
    flat_index = slot_index(block_ids)
    outgoing = dispatch_rows(normed, flat_index)
    per_expert = outgoing.reshape(EXPERTS, CAP, width)
    members = lax.axis_size("ep")
    local_units = w_in.shape[0]
    paired = local_units == 1
    half_cap = CAP // 2
    if paired:
        sending = per_expert.reshape(members, half_cap, width)
    else:
        sending = per_expert
    received = lax.all_to_all(sending, "ep", split_axis=0, concat_axis=1, tiled=True)
    if paired:
        parity = lax.axis_index("ep") % 2
        partner = swapped(received, "ep", 0)
        own_blocks = received.reshape(members, half_cap, width)
        other_blocks = partner.reshape(members, half_cap, width)
        lower = jnp.where(parity == 0, own_blocks, other_blocks)
        upper = jnp.where(parity == 0, other_blocks, own_blocks)
        incoming = jnp.stack([lower, upper], axis=1).reshape(1, members * CAP, width)
    else:
        incoming = jnp.repeat(received, SPLIT, axis=0)
    produced = expert_compute(incoming, w_in, b_in, w_out)
    if paired:
        halves = produced.reshape(members, 2, half_cap, width)
        kept_rows = jnp.where(parity == 0, halves[:, 0], halves[:, 1])
        given_rows = jnp.where(parity == 0, halves[:, 1], halves[:, 0])
        partner_out = swapped(given_rows, "ep", 0)
        reply = (kept_rows.astype(jnp.float32) + partner_out.astype(jnp.float32)).astype(
            jnp.bfloat16
        )
    else:
        local_experts = local_units // SPLIT
        summed = jnp.sum(
            produced.astype(jnp.float32).reshape(local_experts, SPLIT, members, CAP, width), axis=1
        )
        reply = (
            summed.astype(jnp.bfloat16)
            .transpose(1, 0, 2, 3)
            .reshape(members, local_experts * CAP, width)
        )
    returned = lax.all_to_all(reply, "ep", split_axis=0, concat_axis=0, tiled=True)
    expert_out = returned.reshape(EXPERTS, CAP, width)
    result = combine(
        tokens,
        normed,
        settings[2],
        router_weight,
        block_ids,
        flat_index,
        expert_out.reshape(EXPERTS * CAP, width),
    )
    return result.reshape(1, token_count, width)


LANES = 128
HALF_LANES = 64


def flip(index, bit):
    return index + bit * (1 - 2 * ((index // bit) % 2))


def flipped(index, distance, count):
    bit = 1
    while bit < count:
        if distance & bit:
            index = flip(index, bit)
        bit *= 2
    return index


def expert_kernel(
    sizes, hidden_ref, ids_ref, settings_ref, router_ref, w_in_ref, bias_ref, w_out_ref, out_ref,
    far_hidden, far_ids, far_settings, send, got, rows_in, first_w, second_w, acc, r1_out, r1_in, r2_out, r2_in, r3_out, back,
    far_send, far_recv, w_send, w_recv, second_sem, edge_send, edge_recv,
    t1_send, t1_recv, t2_send, t2_recv, t3_send, t3_recv, t4_send, t4_recv,
    r1_send, r1_recv, r2_send, r2_recv, r3_send, r3_recv,
):
    parts, members, experts, units, cols, span, depth, pieces = sizes
    group = parts * members
    part, member, shard = (lax.axis_index(n) for n in ("parts", "ep", "fs"))

    def block_peer(d):
        return {
            "parts": flipped(part, d // members, parts),
            "ep": flipped(member, d % members, members),
            "fs": shard,
        }

    def shard_peer(bit):
        return {"parts": part, "ep": member, "fs": flipped(shard, bit, 4)}

    def remote(src, dst, send, recv, peer):
        return pltpu.make_async_remote_copy(
            src_ref=src, dst_ref=dst, send_sem=send, recv_sem=recv,
            device_id=peer, device_id_type=pl.DeviceIdType.MESH,
        )

    barrier = pltpu.get_barrier_semaphore()
    peers = [block_peer(d) for d in range(1, group)] + [shard_peer(b) for b in range(1, 4)]
    for peer in peers:
        pl.semaphore_signal(
            barrier, inc=1, device_id=peer, device_id_type=pl.DeviceIdType.MESH
        )
    pl.semaphore_wait(barrier, len(peers))

    even = shard % 2 == 0
    rest = span - LANES

    def strip(u, bit, wide):
        target = flipped(shard, bit, 4)
        start = target // 2 * (2 * cols) + (0 if wide else span)
        start = pl.multiple_of(start, LANES)
        src = w_in_ref.at[part * units + u, :, pl.ds(start, span if wide else rest)]
        rows = pl.ds(pl.multiple_of(shard * depth, 32), depth)
        dst = first_w.at[u, rows, :] if wide else first_w.at[u, rows, pl.ds(LANES, rest)]
        if bit == 0:
            return pltpu.make_async_copy(src, dst, w_recv.at[u, 0])
        return remote(src, dst, w_send.at[u, bit], w_recv.at[u, bit], shard_peer(bit))

    def strips_start(u):
        @pl.when(even)
        def _():
            for bit in (2, 3, 1, 0):
                strip(u, bit, bit % 2 == 0).start()

        @pl.when(shard % 2 == 1)
        def _():
            for bit in (2, 3, 1, 0):
                strip(u, bit, bit % 2 == 1).start()

    def edge(u):
        return remote(
            w_out_ref.at[part * units + u, pl.ds(0, HALF_LANES), :],
            second_w.at[u, pl.ds(cols, HALF_LANES), :],
            edge_send.at[u], edge_recv.at[u], shard_peer(1),
        )

    def second_even(u):
        return pltpu.make_async_copy(
            w_out_ref.at[part * units + u], second_w.at[u, pl.ds(0, cols), :], second_sem.at[u]
        )

    def second_odd(u):
        return pltpu.make_async_copy(
            w_out_ref.at[part * units + u, pl.ds(HALF_LANES, rest), :],
            second_w.at[u, pl.ds(LANES, rest), :],
            second_sem.at[u],
        )

    def weights_wait(u):
        @pl.when(even)
        def _():
            strip(u, 0, True).wait()
            for bit in (1, 2, 3):
                strip(u, bit, True).wait_recv()
            second_even(u).wait()
            edge(u).wait_recv()

        @pl.when(shard % 2 == 1)
        def _():
            strip(u, 0, False).wait()
            for bit in (1, 2, 3):
                strip(u, bit, False).wait_recv()
            second_odd(u).wait()

    def far(i):
        src = (hidden_ref, ids_ref, settings_ref)[i]
        dst = (far_hidden, far_ids, far_settings)[i]
        return remote(src, dst, far_send.at[i], far_recv.at[i], shard_peer(2))

    def t1(d):
        if d == 0:
            return pltpu.make_async_copy(send.at[0, 0], got.at[0, 0], t1_recv.at[0])
        return remote(
            send.at[0, d], got.at[0, d], t1_send.at[d], t1_recv.at[d], block_peer(d)
        )

    def t2(d):
        if d == 0:
            return pltpu.make_async_copy(send.at[1, 0], got.at[2, 0], t2_recv.at[0])
        return remote(
            send.at[1, d], got.at[2, d], t2_send.at[d], t2_recv.at[d], block_peer(d)
        )

    def t3(d):
        return remote(got.at[0, d], got.at[1, d], t3_send.at[d], t3_recv.at[d], shard_peer(1))

    def t4(d):
        return remote(got.at[2, d], got.at[3, d], t4_send.at[d], t4_recv.at[d], shard_peer(1))

    def r1(e):
        return remote(r1_out.at[e], r1_in.at[e], r1_send.at[e], r1_recv.at[e], shard_peer(1))

    def r2(e, i):
        return remote(
            r2_out.at[e, i], r2_in.at[e, i], r2_send.at[e, i], r2_recv.at[e, i], shard_peer(2)
        )

    def r3(e, d):
        src, dst = r3_out.at[e, d], back.at[e, d]
        if d == 0:
            return pltpu.make_async_copy(src, dst, r3_recv.at[e, 0])
        return remote(src, dst, r3_send.at[e, d], r3_recv.at[e, d], block_peer(d))

    for i in range(3):
        far(i).start()
    for u in range(units):
        strips_start(u)

    @pl.when(even)
    def _():
        for u in range(units):
            second_even(u).start()

    @pl.when(shard % 2 == 1)
    def _():
        for u in range(units):
            edge(u).start()
            second_odd(u).start()
            first_w[u, :, 0:LANES] = jnp.zeros((first_w.shape[1], LANES), first_w.dtype)
            second_w[u, 0:LANES, :] = jnp.zeros((LANES, second_w.shape[2]), second_w.dtype)

    f32, bf16 = jnp.float32, jnp.bfloat16
    tokens = hidden_ref[...]
    count = tokens.shape[0]
    expert_rows = lax.broadcasted_iota(jnp.int32, (EXPERTS, count), 0)
    before = (
        lax.broadcasted_iota(jnp.int32, (count, count), 0)
        < lax.broadcasted_iota(jnp.int32, (count, count), 1)
    ).astype(f32).astype(bf16)
    own_index = part * members + member
    total_rows = group * experts * CAP
    place_rows = lax.broadcasted_iota(jnp.int32, (total_rows, count), 0)

    def dispatch(image, tokens, ids_ref, settings_ref):
        normed = modulate(tokens, settings_ref[0], settings_ref[1])
        ids = [ids_ref[k : k + 1, :] for k in range(2)]
        hot = [(expert_rows == ids[k]).astype(f32) for k in range(2)]
        earlier = jnp.dot((hot[0] + hot[1]).astype(bf16), before, preferred_element_type=f32)
        slots = [
            jnp.sum(earlier * hot[k], axis=0, keepdims=True).astype(jnp.int32) for k in range(2)
        ]
        holder = [
            ((i // experts % parts) * members + i // (parts * experts)) ^ own_index for i in ids
        ]
        at_holder = [i % experts for i in ids]
        select = sum(
            (place_rows == (holder[k] * experts + at_holder[k]) * CAP + slots[k]).astype(f32)
            for k in range(2)
        )
        outgoing = jnp.dot(select.astype(bf16), normed, preferred_element_type=f32).astype(bf16)
        for d in range(group):
            send[image, d] = outgoing[d * experts * CAP : (d + 1) * experts * CAP]
        return normed, hot, holder, at_holder, slots

    normed, hot, holder, at_holder, slots = dispatch(0, tokens, ids_ref, settings_ref)
    for d in range(group):
        t1(d).start()
    for i in range(3):
        far(i).wait_recv()
    dispatch(1, far_hidden[...], far_ids, far_settings)
    for d in range(group):
        t2(d).start()

    logits = lax.dot_general(
        router_ref[...], normed, (((1,), (1,)), ((), ())), preferred_element_type=f32
    )
    chosen = [jnp.sum(logits * hot[k], axis=0, keepdims=True) for k in range(2)]
    gap = jnp.broadcast_to(chosen[0] - chosen[1], (count, count)).T[:, 0:1]
    mix = [jax.nn.sigmoid(gap), jax.nn.sigmoid(-gap)]
    places = [(at_holder[k] * group + holder[k]) * CAP + slots[k] for k in range(2)]

    def arrived(copy, d):
        if d == 0:
            copy.wait()
        else:
            copy.wait_recv()

    for d in range(group):
        arrived(t1(d), d)
        t3(d).start()
    for d in range(group):
        arrived(t2(d), d)
        t4(d).start()

    half = group * CAP
    batch = 4 if group % 4 == 0 else 1

    def arrange(images, side):
        for place, image in enumerate(images):
            for low in range(0, group, batch):
                chunks = [got[image, low + i] for i in range(batch)]
                for e in range(experts):
                    rows_in[e, side, pl.ds(place * half + low * CAP, batch * CAP), :] = (
                        jnp.concatenate([c[e * CAP : (e + 1) * CAP] for c in chunks], axis=0)
                    )

    arrange((0, 2), 0)
    for d in range(group):
        t3(d).wait_recv()
        t4(d).wait_recv()
    arrange((1, 3), 1)

    piece = half // pieces
    in_piece = group // pieces

    def reply(e):
        for i in range(pieces):
            r2(e, i).wait_recv()
            total = acc[e, 0, i * piece : (i + 1) * piece, :] + r2_in[e, i].astype(f32)
            total = total.astype(bf16)
            for j in range(in_piece):
                r3_out[e, i * in_piece + j] = total[j * CAP : (j + 1) * CAP]
            for j in range(in_piece):
                r3(e, i * in_piece + j).start()

    def picked(e):
        for d in range(group):
            arrived(r3(e, d), d)
        rows = jnp.concatenate([back[e, d] for d in range(group)], axis=0)
        columns = lax.broadcasted_iota(jnp.int32, (half, count), 0) + e * half
        branch = 0.0
        for k in range(2):
            pick = (columns == places[k]).astype(f32).astype(bf16)
            branch = branch + mix[k] * lax.dot_general(
                pick, rows, (((0,), (0,)), ((), ())), preferred_element_type=f32
            )
        return branch

    for e in range(experts):
        for p in range(SPLIT):
            u = e * SPLIT + p
            weights_wait(u)
            start = pl.multiple_of(shard // 2 * (2 * cols) + shard % 2 * (span - LANES), LANES)
            bias = bias_ref[pl.ds(part * units + u, 1), pl.ds(start, span)]
            for side in (1, 0):
                pre = jnp.dot(
                    rows_in[e, side], first_w[u], preferred_element_type=jnp.float32
                )
                hidden = jax.nn.gelu(pre + bias, approximate=True).astype(jnp.bfloat16)
                made = jnp.dot(hidden, second_w[u], preferred_element_type=jnp.float32)
                if p > 0:
                    made = made + acc[e, side]
                if p == SPLIT - 1 and side == 1:
                    r1_out[e] = made.astype(jnp.bfloat16)
                    r1(e).start()
                else:
                    acc[e, side] = made
            if p == 0 and e > 0:
                reply(e - 1)
        r1(e).wait_recv()
        chip = acc[e, 0] + r1_in[e].astype(jnp.float32)
        for i in range(pieces):
            r2_out[e, i] = chip[half + i * piece : half + (i + 1) * piece].astype(bf16)
        for i in range(pieces):
            r2(e, i).start()
        acc[e, 0] = chip
    reply(experts - 1)

    branch = sum(picked(e) for e in range(experts))
    out_ref[...] = (tokens.astype(f32) + settings_ref[2] * branch).astype(bf16)

    for e in range(experts):
        for d in range(1, group):
            r3(e, d).wait_send()
        r1(e).wait_send()
        for i in range(pieces):
            r2(e, i).wait_send()

    for i in range(3):
        far(i).wait_send()

    @pl.when(even)
    def _():
        for u in range(units):
            for bit in (1, 2, 3):
                strip(u, bit, bit % 2 == 0).wait_send()

    @pl.when(shard % 2 == 1)
    def _():
        for u in range(units):
            edge(u).wait_send()
            for bit in (1, 2, 3):
                strip(u, bit, bit % 2 == 1).wait_send()

    for d in range(group):
        if d > 0:
            t1(d).wait_send()
            t2(d).wait_send()
        t3(d).wait_send()
        t4(d).wait_send()


def local_spread(hidden_states, expert_ids, modulation, router_weight, w_in, b_in, w_out):
    token_count = hidden_states.shape[1]
    width = hidden_states.shape[2]
    parts, members, shards = (lax.axis_size(a) for a in ("parts", "ep", "fs"))
    group = parts * members
    units = w_in.shape[0] // parts
    experts = units // SPLIT
    depth = w_in.shape[1]
    cols = w_in.shape[2] // shards
    span = cols + cols % LANES
    pieces = 4 if group % 4 == 0 else 1

    rows = 2 * group * CAP
    bf16, dma = jnp.bfloat16, pltpu.SemaphoreType.DMA
    hbm, vmem = pl.BlockSpec(memory_space=pl.ANY), pl.BlockSpec(memory_space=pltpu.VMEM)
    sizes = (parts, members, experts, units, cols, span, depth, pieces)
    result = pl.pallas_call(
        functools.partial(expert_kernel, sizes),
        out_shape=jax.ShapeDtypeStruct((token_count, width), bf16),
        in_specs=[vmem, vmem, vmem, vmem, hbm, vmem, hbm],
        out_specs=vmem,
        scratch_shapes=[
            pltpu.VMEM((token_count, width), bf16),
            pltpu.VMEM((2, token_count), jnp.int32),
            pltpu.VMEM((modulation.shape[1], 1, width), jnp.float32),
            pltpu.VMEM((2, group, experts * CAP, width), bf16),
            pltpu.VMEM((shards, group, experts * CAP, width), bf16),
            pltpu.VMEM((experts, 2, rows, width), bf16),
            pltpu.VMEM((units, width, span), bf16),
            pltpu.VMEM((units, span, width), bf16),
            pltpu.VMEM((experts, 2, rows, width), jnp.float32),
            pltpu.VMEM((experts, rows, width), bf16),
            pltpu.VMEM((experts, rows, width), bf16),
            pltpu.VMEM((experts, pieces, rows // 2 // pieces, width), bf16),
            pltpu.VMEM((experts, pieces, rows // 2 // pieces, width), bf16),
            pltpu.VMEM((experts, group, CAP, width), bf16),
            pltpu.VMEM((experts, group, CAP, width), bf16),
            dma((3,)), dma((3,)),
            dma((units, 4)), dma((units, 4)), dma((units,)),
            dma((units,)), dma((units,)),
        ]
        + [dma((group,))] * 8
        + [dma((experts,))] * 2
        + [dma((experts, pieces))] * 2
        + [dma((experts, group))] * 2,
        compiler_params=pltpu.CompilerParams(
            collective_id=0, has_side_effects=True, vmem_limit_bytes=60 * 1024 * 1024
        ),
    )(
        hidden_states.reshape(token_count, width),
        expert_ids.reshape(token_count, 2).T,
        modulation.transpose(1, 0, 2),
        router_weight.T,
        w_in,
        b_in,
        w_out,
    )
    return result.reshape(1, token_count, width)


def solution(mesh):
    sizes = mesh.shape
    group = sizes["ep"] * sizes["parts"]
    spread = sizes["fs"] == 4 and EXPERTS % group == 0 and sizes["parts"] == 2
    placed = (
        P(("parts", "fs"), "ep", None),
        P(("parts", "fs"), "ep", None),
        P(("parts", "fs"), None, None),
        P(),
        P("ep", "fs", None),
        P("ep", None),
        P("ep", "fs", None),
    )
    return jax.shard_map(
        local_spread if spread else local, mesh=mesh, in_specs=placed, out_specs=P(("parts", "fs"), "ep", None), check_vma=False
    )
```

```python
import functools

import jax
import jax.numpy as jnp
from jax import lax
from jax.experimental import pallas as pl
from jax.experimental.pallas import tpu as pltpu
from jax.sharding import PartitionSpec as P

EXPERTS = 16
SPLIT = 2
CAP = 20


norm_eps = 1e-06


def swapped(block, axis, distance):
    count = lax.axis_size(axis)
    route = []
    for low in range(count):
        high = low | 1 << distance
        if high != low and high < count:
            route += [(low, high), (high, low)]
    return lax.ppermute(block, axis, route)


def modulate(tokens, shift, scale):
    values = tokens.astype(jnp.float32)
    center = jnp.mean(values, axis=-1, keepdims=True)
    spread = jnp.mean(jnp.square(values - center), axis=-1, keepdims=True)
    normal = (values - center) * lax.rsqrt(spread + norm_eps)
    return (normal * (1.0 + scale) + shift).astype(jnp.bfloat16)


def slot_index(block_ids):
    flat_ids = block_ids.reshape(-1)
    one_hot = (flat_ids[:, None] == jnp.arange(EXPERTS, dtype=jnp.int32)[None, :]).astype(jnp.int32)
    earlier = jnp.cumsum(one_hot, axis=0, dtype=jnp.int32) - one_hot
    slots = jnp.sum(earlier * one_hot, axis=1, dtype=jnp.int32)
    return (flat_ids * CAP + slots).reshape(block_ids.shape)


def dispatch_rows(normed, flat_index):
    targets = jnp.arange(EXPERTS * CAP, dtype=jnp.int32)
    select = jnp.sum(
        (flat_index[None, :, :] == targets[:, None, None]).astype(jnp.int32),
        axis=2,
        dtype=jnp.int32,
    )
    return jnp.dot(select.astype(jnp.bfloat16), normed, preferred_element_type=jnp.float32).astype(
        jnp.bfloat16
    )


def combine(tokens, normed, gate_row, router_weight, block_ids, flat_index, expert_out):
    logits = jnp.dot(normed, router_weight, preferred_element_type=jnp.float32)
    picked = jnp.take_along_axis(logits, block_ids, axis=1)
    gap = picked[:, 0:1] - picked[:, 1:2]
    first = jnp.take(expert_out, flat_index[:, 0], axis=0).astype(jnp.float32)
    second = jnp.take(expert_out, flat_index[:, 1], axis=0).astype(jnp.float32)
    branch = jax.nn.sigmoid(gap) * first + jax.nn.sigmoid(-gap) * second
    return (tokens.astype(jnp.float32) + gate_row[None, :] * branch).astype(jnp.bfloat16)


def expert_compute(incoming, w_in, b_in, w_out):
    columns = incoming
    pre_act = jnp.einsum(
        "urd,udf->urf",
        columns,
        lax.all_gather(w_in, "fs", axis=1, tiled=True),
        preferred_element_type=jnp.float32,
    )
    hidden = jax.nn.gelu(pre_act + b_in[:, None, :], approximate=True).astype(jnp.bfloat16)
    columns = hidden
    produced = jnp.einsum(
        "urf,ufd->urd",
        columns,
        lax.all_gather(w_out, "fs", axis=1, tiled=True),
        preferred_element_type=jnp.float32,
    )
    return produced.astype(jnp.bfloat16)


def local(hidden_states, expert_ids, modulation, router_weight, w_in, b_in, w_out):
    token_count = hidden_states.shape[1]
    width = hidden_states.shape[2]
    tokens = hidden_states.reshape(token_count, width)
    block_ids = expert_ids.reshape(token_count, 2)
    settings = modulation[0]
    normed = modulate(tokens, settings[0][None, :], settings[1][None, :])
    flat_index = slot_index(block_ids)
    outgoing = dispatch_rows(normed, flat_index)
    per_expert = outgoing.reshape(EXPERTS, CAP, width)
    members = lax.axis_size("ep")
    local_units = w_in.shape[0]
    paired = local_units == 1
    half_cap = CAP // 2
    if paired:
        sending = per_expert.reshape(members, half_cap, width)
    else:
        sending = per_expert
    received = lax.all_to_all(sending, "ep", split_axis=0, concat_axis=1, tiled=True)
    if paired:
        parity = lax.axis_index("ep") % 2
        partner = swapped(received, "ep", 0)
        own_blocks = received.reshape(members, half_cap, width)
        other_blocks = partner.reshape(members, half_cap, width)
        lower = jnp.where(parity == 0, own_blocks, other_blocks)
        upper = jnp.where(parity == 0, other_blocks, own_blocks)
        incoming = jnp.stack([lower, upper], axis=1).reshape(1, members * CAP, width)
    else:
        incoming = jnp.repeat(received, SPLIT, axis=0)
    produced = expert_compute(incoming, w_in, b_in, w_out)
    if paired:
        halves = produced.reshape(members, 2, half_cap, width)
        kept_rows = jnp.where(parity == 0, halves[:, 0], halves[:, 1])
        given_rows = jnp.where(parity == 0, halves[:, 1], halves[:, 0])
        partner_out = swapped(given_rows, "ep", 0)
        reply = (kept_rows.astype(jnp.float32) + partner_out.astype(jnp.float32)).astype(
            jnp.bfloat16
        )
    else:
        local_experts = local_units // SPLIT
        summed = jnp.sum(
            produced.astype(jnp.float32).reshape(local_experts, SPLIT, members, CAP, width), axis=1
        )
        reply = (
            summed.astype(jnp.bfloat16)
            .transpose(1, 0, 2, 3)
            .reshape(members, local_experts * CAP, width)
        )
    returned = lax.all_to_all(reply, "ep", split_axis=0, concat_axis=0, tiled=True)
    expert_out = returned.reshape(EXPERTS, CAP, width)
    result = combine(
        tokens,
        normed,
        settings[2],
        router_weight,
        block_ids,
        flat_index,
        expert_out.reshape(EXPERTS * CAP, width),
    )
    return result.reshape(1, token_count, width)


LANES = 128
HALF_LANES = 64


def flip(index, bit):
    return index + bit * (1 - 2 * ((index // bit) % 2))


def flipped(index, distance, count):
    bit = 1
    while bit < count:
        if distance & bit:
            index = flip(index, bit)
        bit *= 2
    return index


def expert_kernel(
    sizes, hidden_ref, ids_ref, settings_ref, router_ref, w_in_ref, bias_ref, w_out_ref, out_ref,
    far_hidden, far_ids, far_settings, send, got, rows_in, first_w, second_w, acc, r1_out, r1_in, r2_out, r2_in, r3_out, back,
    far_send, far_recv, w_send, w_recv, second_sem, edge_send, edge_recv,
    t1_send, t1_recv, t2_send, t2_recv, t3_send, t3_recv, t4_send, t4_recv,
    r1_send, r1_recv, r2_send, r2_recv, r3_send, r3_recv,
):
    parts, members, experts, units, cols, span, depth, pieces = sizes
    group = parts * members
    part, member, shard = (lax.axis_index(n) for n in ("parts", "ep", "fs"))

    def block_peer(d):
        return {
            "parts": flipped(part, d // members, parts),
            "ep": flipped(member, d % members, members),
            "fs": shard,
        }

    def shard_peer(bit):
        return {"parts": part, "ep": member, "fs": flipped(shard, bit, 4)}

    def remote(src, dst, send, recv, peer):
        return pltpu.make_async_remote_copy(
            src_ref=src, dst_ref=dst, send_sem=send, recv_sem=recv,
            device_id=peer, device_id_type=pl.DeviceIdType.MESH,
        )

    barrier = pltpu.get_barrier_semaphore()
    peers = [block_peer(d) for d in range(1, group)] + [shard_peer(b) for b in range(1, 4)]
    for peer in peers:
        pl.semaphore_signal(
            barrier, inc=1, device_id=peer, device_id_type=pl.DeviceIdType.MESH
        )
    pl.semaphore_wait(barrier, len(peers))

    even = shard % 2 == 0
    rest = span - LANES

    def strip(u, bit, wide):
        target = flipped(shard, bit, 4)
        start = target // 2 * (2 * cols) + (0 if wide else span)
        start = pl.multiple_of(start, LANES)
        src = w_in_ref.at[part * units + u, :, pl.ds(start, span if wide else rest)]
        rows = pl.ds(pl.multiple_of(shard * depth, 32), depth)
        dst = first_w.at[u, rows, :] if wide else first_w.at[u, rows, pl.ds(LANES, rest)]
        if bit == 0:
            return pltpu.make_async_copy(src, dst, w_recv.at[u, 0])
        return remote(src, dst, w_send.at[u, bit], w_recv.at[u, bit], shard_peer(bit))

    def strips_start(u):
        @pl.when(even)
        def _():
            for bit in (2, 3, 1, 0):
                strip(u, bit, bit % 2 == 0).start()

        @pl.when(shard % 2 == 1)
        def _():
            for bit in (2, 3, 1, 0):
                strip(u, bit, bit % 2 == 1).start()

    def edge(u):
        return remote(
            w_out_ref.at[part * units + u, pl.ds(0, HALF_LANES), :],
            second_w.at[u, pl.ds(cols, HALF_LANES), :],
            edge_send.at[u], edge_recv.at[u], shard_peer(1),
        )

    def second_even(u):
        return pltpu.make_async_copy(
            w_out_ref.at[part * units + u], second_w.at[u, pl.ds(0, cols), :], second_sem.at[u]
        )

    def second_odd(u):
        return pltpu.make_async_copy(
            w_out_ref.at[part * units + u, pl.ds(HALF_LANES, rest), :],
            second_w.at[u, pl.ds(LANES, rest), :],
            second_sem.at[u],
        )

    def weights_wait(u):
        @pl.when(even)
        def _():
            strip(u, 0, True).wait()
            for bit in (1, 2, 3):
                strip(u, bit, True).wait_recv()
            second_even(u).wait()
            edge(u).wait_recv()

        @pl.when(shard % 2 == 1)
        def _():
            strip(u, 0, False).wait()
            for bit in (1, 2, 3):
                strip(u, bit, False).wait_recv()
            second_odd(u).wait()

    def far(i):
        src = (hidden_ref, ids_ref, settings_ref)[i]
        dst = (far_hidden, far_ids, far_settings)[i]
        return remote(src, dst, far_send.at[i], far_recv.at[i], shard_peer(2))

    def t1(d):
        if d == 0:
            return pltpu.make_async_copy(send.at[0, 0], got.at[0, 0], t1_recv.at[0])
        return remote(
            send.at[0, d], got.at[0, d], t1_send.at[d], t1_recv.at[d], block_peer(d)
        )

    def t2(d):
        if d == 0:
            return pltpu.make_async_copy(send.at[1, 0], got.at[2, 0], t2_recv.at[0])
        return remote(
            send.at[1, d], got.at[2, d], t2_send.at[d], t2_recv.at[d], block_peer(d)
        )

    def t3(d):
        return remote(got.at[0, d], got.at[1, d], t3_send.at[d], t3_recv.at[d], shard_peer(1))

    def t4(d):
        return remote(got.at[2, d], got.at[3, d], t4_send.at[d], t4_recv.at[d], shard_peer(1))

    def r1(e):
        return remote(r1_out.at[e], r1_in.at[e], r1_send.at[e], r1_recv.at[e], shard_peer(1))

    def r2(e, i):
        return remote(
            r2_out.at[e, i], r2_in.at[e, i], r2_send.at[e, i], r2_recv.at[e, i], shard_peer(2)
        )

    def r3(e, d):
        src, dst = r3_out.at[e, d], back.at[e, d]
        if d == 0:
            return pltpu.make_async_copy(src, dst, r3_recv.at[e, 0])
        return remote(src, dst, r3_send.at[e, d], r3_recv.at[e, d], block_peer(d))

    for i in range(3):
        far(i).start()
    for u in range(units):
        strips_start(u)

    @pl.when(even)
    def _():
        for u in range(units):
            second_even(u).start()

    @pl.when(shard % 2 == 1)
    def _():
        for u in range(units):
            edge(u).start()
            second_odd(u).start()
            first_w[u, :, 0:LANES] = jnp.zeros((first_w.shape[1], LANES), first_w.dtype)
            second_w[u, 0:LANES, :] = jnp.zeros((LANES, second_w.shape[2]), second_w.dtype)

    f32, bf16 = jnp.float32, jnp.bfloat16
    tokens = hidden_ref[...]
    count = tokens.shape[0]
    expert_rows = lax.broadcasted_iota(jnp.int32, (EXPERTS, count), 0)
    before = (
        lax.broadcasted_iota(jnp.int32, (count, count), 0)
        < lax.broadcasted_iota(jnp.int32, (count, count), 1)
    ).astype(f32).astype(bf16)
    own_index = part * members + member
    total_rows = group * experts * CAP
    place_rows = lax.broadcasted_iota(jnp.int32, (total_rows, count), 0)

    def dispatch(image, tokens, ids_ref, settings_ref):
        normed = modulate(tokens, settings_ref[0], settings_ref[1])
        ids = [ids_ref[k : k + 1, :] for k in range(2)]
        hot = [(expert_rows == ids[k]).astype(f32) for k in range(2)]
        earlier = jnp.dot((hot[0] + hot[1]).astype(bf16), before, preferred_element_type=f32)
        slots = [
            jnp.sum(earlier * hot[k], axis=0, keepdims=True).astype(jnp.int32) for k in range(2)
        ]
        holder = [
            ((i // experts % parts) * members + i // (parts * experts)) ^ own_index for i in ids
        ]
        at_holder = [i % experts for i in ids]
        select = sum(
            (place_rows == (holder[k] * experts + at_holder[k]) * CAP + slots[k]).astype(f32)
            for k in range(2)
        )
        outgoing = jnp.dot(select.astype(bf16), normed, preferred_element_type=f32).astype(bf16)
        for d in range(group):
            send[image, d] = outgoing[d * experts * CAP : (d + 1) * experts * CAP]
        return normed, hot, holder, at_holder, slots

    normed, hot, holder, at_holder, slots = dispatch(0, tokens, ids_ref, settings_ref)
    for d in range(group):
        t1(d).start()
    for i in range(3):
        far(i).wait_recv()
    dispatch(1, far_hidden[...], far_ids, far_settings)
    for d in range(group):
        t2(d).start()

    logits = lax.dot_general(
        router_ref[...], normed, (((1,), (1,)), ((), ())), preferred_element_type=f32
    )
    chosen = [jnp.sum(logits * hot[k], axis=0, keepdims=True) for k in range(2)]
    gap = jnp.broadcast_to(chosen[0] - chosen[1], (count, count)).T[:, 0:1]
    mix = [jax.nn.sigmoid(gap), jax.nn.sigmoid(-gap)]
    places = [(at_holder[k] * group + holder[k]) * CAP + slots[k] for k in range(2)]

    def arrived(copy, d):
        if d == 0:
            copy.wait()
        else:
            copy.wait_recv()

    for d in range(group):
        arrived(t1(d), d)
        t3(d).start()
    for d in range(group):
        arrived(t2(d), d)
        t4(d).start()

    half = group * CAP
    batch = 4 if group % 4 == 0 else 1

    def arrange(images, side):
        for place, image in enumerate(images):
            for low in range(0, group, batch):
                chunks = [got[image, low + i] for i in range(batch)]
                for e in range(experts):
                    rows_in[e, side, pl.ds(place * half + low * CAP, batch * CAP), :] = (
                        jnp.concatenate([c[e * CAP : (e + 1) * CAP] for c in chunks], axis=0)
                    )

    arrange((0, 2), 0)
    piece = half // pieces
    in_piece = group // pieces

    def reply(e):
        for i in range(pieces):
            r2(e, i).wait_recv()
            total = acc[e, 0, i * piece : (i + 1) * piece, :] + r2_in[e, i].astype(f32)
            total = total.astype(bf16)
            for j in range(in_piece):
                r3_out[e, i * in_piece + j] = total[j * CAP : (j + 1) * CAP]
            for j in range(in_piece):
                r3(e, i * in_piece + j).start()

    def picked(e):
        for d in range(group):
            arrived(r3(e, d), d)
        rows = jnp.concatenate([back[e, d] for d in range(group)], axis=0)
        columns = lax.broadcasted_iota(jnp.int32, (half, count), 0) + e * half
        branch = 0.0
        for k in range(2):
            pick = (columns == places[k]).astype(f32).astype(bf16)
            branch = branch + mix[k] * lax.dot_general(
                pick, rows, (((0,), (0,)), ((), ())), preferred_element_type=f32
            )
        return branch

    for e in range(experts):
        for p in range(SPLIT):
            u = e * SPLIT + p
            weights_wait(u)
            start = pl.multiple_of(shard // 2 * (2 * cols) + shard % 2 * (span - LANES), LANES)
            bias = bias_ref[pl.ds(part * units + u, 1), pl.ds(start, span)]
            for side in (1, 0) if p > 0 else (0, 1):
                if u == 0 and side == 1:
                    for d in range(group):
                        t3(d).wait_recv()
                        t4(d).wait_recv()
                    arrange((1, 3), 1)
                pre = jnp.dot(
                    rows_in[e, side], first_w[u], preferred_element_type=jnp.float32
                )
                hidden = jax.nn.gelu(pre + bias, approximate=True).astype(jnp.bfloat16)
                made = jnp.dot(hidden, second_w[u], preferred_element_type=jnp.float32)
                if p > 0:
                    made = made + acc[e, side]
                if p == SPLIT - 1 and side == 1:
                    r1_out[e] = made.astype(jnp.bfloat16)
                    r1(e).start()
                else:
                    acc[e, side] = made
            if p == 0 and e > 0:
                reply(e - 1)
        r1(e).wait_recv()
        chip = acc[e, 0] + r1_in[e].astype(jnp.float32)
        for i in range(pieces):
            r2_out[e, i] = chip[half + i * piece : half + (i + 1) * piece].astype(bf16)
        for i in range(pieces):
            r2(e, i).start()
        acc[e, 0] = chip
    reply(experts - 1)

    branch = sum(picked(e) for e in range(experts))
    out_ref[...] = (tokens.astype(f32) + settings_ref[2] * branch).astype(bf16)

    for e in range(experts):
        for d in range(1, group):
            r3(e, d).wait_send()
        r1(e).wait_send()
        for i in range(pieces):
            r2(e, i).wait_send()

    for i in range(3):
        far(i).wait_send()

    @pl.when(even)
    def _():
        for u in range(units):
            for bit in (1, 2, 3):
                strip(u, bit, bit % 2 == 0).wait_send()

    @pl.when(shard % 2 == 1)
    def _():
        for u in range(units):
            edge(u).wait_send()
            for bit in (1, 2, 3):
                strip(u, bit, bit % 2 == 1).wait_send()

    for d in range(group):
        if d > 0:
            t1(d).wait_send()
            t2(d).wait_send()
        t3(d).wait_send()
        t4(d).wait_send()


def local_spread(hidden_states, expert_ids, modulation, router_weight, w_in, b_in, w_out):
    token_count = hidden_states.shape[1]
    width = hidden_states.shape[2]
    parts, members, shards = (lax.axis_size(a) for a in ("parts", "ep", "fs"))
    group = parts * members
    units = w_in.shape[0] // parts
    experts = units // SPLIT
    depth = w_in.shape[1]
    cols = w_in.shape[2] // shards
    span = cols + cols % LANES
    pieces = 4 if group % 4 == 0 else 1

    rows = 2 * group * CAP
    bf16, dma = jnp.bfloat16, pltpu.SemaphoreType.DMA
    hbm, vmem = pl.BlockSpec(memory_space=pl.ANY), pl.BlockSpec(memory_space=pltpu.VMEM)
    sizes = (parts, members, experts, units, cols, span, depth, pieces)
    result = pl.pallas_call(
        functools.partial(expert_kernel, sizes),
        out_shape=jax.ShapeDtypeStruct((token_count, width), bf16),
        in_specs=[vmem, vmem, vmem, vmem, hbm, vmem, hbm],
        out_specs=vmem,
        scratch_shapes=[
            pltpu.VMEM((token_count, width), bf16),
            pltpu.VMEM((2, token_count), jnp.int32),
            pltpu.VMEM((modulation.shape[1], 1, width), jnp.float32),
            pltpu.VMEM((2, group, experts * CAP, width), bf16),
            pltpu.VMEM((shards, group, experts * CAP, width), bf16),
            pltpu.VMEM((experts, 2, rows, width), bf16),
            pltpu.VMEM((units, width, span), bf16),
            pltpu.VMEM((units, span, width), bf16),
            pltpu.VMEM((experts, 2, rows, width), jnp.float32),
            pltpu.VMEM((experts, rows, width), bf16),
            pltpu.VMEM((experts, rows, width), bf16),
            pltpu.VMEM((experts, pieces, rows // 2 // pieces, width), bf16),
            pltpu.VMEM((experts, pieces, rows // 2 // pieces, width), bf16),
            pltpu.VMEM((experts, group, CAP, width), bf16),
            pltpu.VMEM((experts, group, CAP, width), bf16),
            dma((3,)), dma((3,)),
            dma((units, 4)), dma((units, 4)), dma((units,)),
            dma((units,)), dma((units,)),
        ]
        + [dma((group,))] * 8
        + [dma((experts,))] * 2
        + [dma((experts, pieces))] * 2
        + [dma((experts, group))] * 2,
        compiler_params=pltpu.CompilerParams(
            collective_id=0, has_side_effects=True, vmem_limit_bytes=60 * 1024 * 1024
        ),
    )(
        hidden_states.reshape(token_count, width),
        expert_ids.reshape(token_count, 2).T,
        modulation.transpose(1, 0, 2),
        router_weight.T,
        w_in,
        b_in,
        w_out,
    )
    return result.reshape(1, token_count, width)


def solution(mesh):
    sizes = mesh.shape
    group = sizes["ep"] * sizes["parts"]
    spread = sizes["fs"] == 4 and EXPERTS % group == 0 and sizes["parts"] == 2
    placed = (
        P(("parts", "fs"), "ep", None),
        P(("parts", "fs"), "ep", None),
        P(("parts", "fs"), None, None),
        P(),
        P("ep", "fs", None),
        P("ep", None),
        P("ep", "fs", None),
    )
    return jax.shard_map(
        local_spread if spread else local, mesh=mesh, in_specs=placed, out_specs=P(("parts", "fs"), "ep", None), check_vma=False
    )
```
